32 devices in a mesh: groups: 2 (over y), markov: 4 (over z), storage: 2 (over x), sub: 2 (over core).
Axes of the slice: x: 2, y: 2, z: 4, core: 2. Of those that a mesh axis runs over, the one named last changes fastest.
Arguments:
- expected_cot: bfloat16 [8192, 2048], P(('groups', 'markov'), ('storage', 'sub')), parts along dimension 0, may hold values from -192 to 192
- value_next: bfloat16 [8192, 2048], P(('groups', 'markov'), ('storage', 'sub')), parts along dimension 0, may hold values from -0.0024414062 to 0.0024414062
- transition: bfloat16 [8192, 4096], P(('groups', 'storage', 'sub'), 'markov'), parts along dimension 0, may hold values from 6.1035156e-05 to 0.0009765625
- section: int32 [2], P('groups'), parts along dimension 0, may hold values from 0 to 51
Outputs:
- section_adjoint: float32 [8192, 2048], P(('groups', 'markov'), ('storage', 'sub')), parts along dimension 0
- transition_grad: float32 [8192, 4096], P(('groups', 'storage', 'sub'), 'markov'), parts along dimension 0
The draws below stay inside these ranges and needn't reach their ends.
There are 2 independent parts, one for each index of `groups`. The reference program is written for one: setup_inputs(seed, part) draws one part's arguments, and reference() takes and returns one part's arrays. A program takes and returns all parts, laid end to end along the dimension named above; each array names one. Nothing has to cross between parts.
All inputs are finite; a program needn't handle non-finite values.
Results may differ from the reference program's by a relative error of at most 0.0003.
Values may be sent and summed in bfloat16 or wider, within the bound.
A program may use at most 64 MiB of HBM per device.

```python
import math
import jax
import jax.numpy as jnp
from jax import lax

M = 4096
SECTIONS = 52
CELLS = 2048


def steps_of(own_key, shape, shards, smallest, top_value):
    def one(dim, shards_of):
        heights = jax.random.uniform(jax.random.fold_in(jax.random.fold_in(own_key, 6), dim), (shards_of,), jnp.float32, smallest / len(shards), top_value / len(shards))
        return jnp.repeat(jnp.exp(heights), shape[dim] // shards_of).reshape((-1,) + (1,) * (len(shape) - dim - 1))

    loudness = one(*shards[0])
    for cut in shards[1:]:
        loudness = loudness * one(*cut)
    return loudness


def scatter_about(key, extent, width, reach, split=(), held_as=jnp.bfloat16):
    drawn = width * jax.random.normal(key, extent, jnp.float32)
    if split:
        drawn = drawn * steps_of(key, extent, split, -0.22, 0.18)
    return jnp.clip(drawn, -reach, reach).astype(held_as)


def setup_inputs(seed: int = 0, part: int = 0) -> dict:
    keys = jax.random.split(jax.random.key(seed), 5)
    own_keys = jax.random.split(jax.random.fold_in(keys[4], part), 5)
    expected_cot = scatter_about(own_keys[0], (M, CELLS), 32.0, 192.0, ((0, 4), (1, 4)))
    value_next = scatter_about(own_keys[1], (M, CELLS), 0.0004, 0.0024414062, ((0, 4), (1, 4)))
    transition = jnp.clip(jnp.exp(math.log(0.0009765625) - 2.7725887 * jax.random.uniform(own_keys[2], (M, M), jnp.float32) ** steps_of(own_keys[2], (M, M), ((0, 4), (1, 4)), -0.2, 0.2)), 6.103515625e-05, 0.0009765625).astype(jnp.bfloat16)
    section = jax.random.randint(own_keys[3], (1,), 0, SECTIONS).astype(jnp.int32)
    return {"expected_cot": expected_cot, "value_next": value_next, "transition": transition, "section": section}


discount_rate = 0.97


def reference(expected_cot, value_next, transition, section):
    discount_factor = jnp.exp(section[0].astype(jnp.float32) * jnp.log(jnp.float32(discount_rate)))
    adjoint_sum = lax.dot_general(transition, expected_cot, (((0,), (0,)), ((), ())), preferred_element_type=jnp.float32)
    gradient_sum = lax.dot_general(expected_cot, value_next, (((1,), (1,)), ((), ())), preferred_element_type=jnp.float32)
    return discount_factor * adjoint_sum, discount_factor * gradient_sum
```

```python
import jax
import jax.numpy as jnp
from jax import lax
from jax.experimental import pallas as pl
from jax.experimental.pallas import tpu as pltpu
from jax.sharding import PartitionSpec as P

discount_rate = 0.97
MESH = pl.DeviceIdType.MESH
PIECES = 2
TILE = 256
VMEM_BYTES = 40 * 1024 * 1024


def discount_of(section):
    return jnp.exp(section[0].astype(jnp.float32) * jnp.log(jnp.float32(discount_rate)))


def gathered(expected_cot, value_next, transition, section):
    discount_factor = discount_of(section)
    cotangent_all = lax.all_gather(expected_cot, "markov", axis=0, tiled=True)
    adjoint_sum = lax.dot_general(
        lax.all_gather(transition, ("storage", "sub"), axis=0, tiled=True),
        cotangent_all,
        (((0,), (0,)), ((), ())),
        preferred_element_type=jnp.float32,
    )
    own_states = lax.all_to_all(
        cotangent_all, ("storage", "sub"), split_axis=0, concat_axis=1, tiled=True
    )
    gathered_values = lax.all_gather(value_next, ("storage", "sub"), axis=1, tiled=True)
    gradient_sum = lax.dot_general(
        own_states, gathered_values, (((1,), (1,)), ((), ())), preferred_element_type=jnp.float32
    )
    return (discount_factor * adjoint_sum, discount_factor * gradient_sum)


def kernel(
    c_in, v_in, t_in, adj, grad, c_all, c_pair, t_own, t_pair, v_all, p_out, p_in,
    c_recv, up_send, down_send, own_send, own_extra, pair_send, pair_recv,
    v_send, v_recv, t_sems, p_send, p_recv,
):
    g, m = lax.axis_index("groups"), lax.axis_index("markov")
    s, u = lax.axis_index("storage"), lax.axis_index("sub")
    far = 1 - s
    j, p, o, q = 2 * s + u, 2 * s + 1 - u, 2 * far + u, 2 * far + 1 - u
    step = 1 - 2 * s
    z = m + s * (3 - 2 * m)
    row = u + s * (1 - 2 * u)
    partner, across = (g, m, s, 1 - u), (g, m, far, u)
    above, below = (g, jnp.clip(m + step, 0, 3), s, u), (g, jnp.clip(m - step, 0, 3), s, u)
    home = lax.rem(m, 2)
    states, half = c_all.shape[1:]
    tall = states // PIECES
    following = grad.shape[1]
    is_a, is_b = (z <= 1) & (row == z), (z <= 1) & (row != z)
    is_far = z >= 2

    def remote(src, dst, send, recv, to):
        return pltpu.make_async_remote_copy(
            src_ref=src, dst_ref=dst, send_sem=send, recv_sem=recv, device_id=to, device_id_type=MESH
        )

    def held(k, r):
        return c_all.at[k, pl.ds(r * tall, tall)]

    def mine(h, r):
        return c_in.at[pl.ds(r * tall, tall), pl.ds(h * half, half)]

    def got(k, r):
        remote(held(k, r), held(k, r), c_recv.at[k, r], c_recv.at[k, r], partner).wait_recv()

    def z_copy(k, r, send, to):
        return remote(held(k, r), held(k, r), send.at[k, r], c_recv.at[k, r], to)

    def own_copy(h, r, send, to):
        return remote(mine(h, r), held(2 * j + h, r), send.at[h, r], c_recv.at[2 * j + h, r], to)

    up_home = (g, jnp.clip(m + step, 0, 3), s, home)
    down_home = (g, jnp.clip(m - step, 0, 3), s, home)

    def far_home(h):
        return (g, jnp.clip(m - step * (h + 3 - z), 0, 3), far, home)

    def own_up(h, r):
        return own_copy(h, r, own_send, up_home)

    def own_down(h, r):
        return own_copy(h, r, own_extra, down_home)

    def own_far(h, r):
        return own_copy(h, r, own_send, far_home(h))

    def own_pair(h, r):
        return own_copy(h, r, own_extra.at[pl.ds(2, 2)], partner)

    def pair_copy(i, k):
        return remote(c_all.at[k], c_pair.at[i], pair_send.at[i], pair_recv.at[i], partner)

    v_tall = states // 2

    def v_across(i):
        at = pl.ds(i * v_tall, v_tall)
        return remote(v_in.at[at], v_all.at[j, at], v_send.at[i], v_recv.at[i], across)

    def v_relay():
        return remote(v_all.at[o], v_all.at[o], v_send.at[2], v_recv.at[2], partner)

    def v_pair():
        return remote(v_in, v_all.at[j], v_send.at[3], v_recv.at[3], partner)

    def t_copy():
        return remote(t_in, t_pair, t_sems.at[0], t_sems.at[1], partner)

    def p_copy(h, i):
        at = pl.ds(pl.multiple_of(i * TILE, TILE), TILE)
        return remote(p_out.at[h, at], p_in.at[h, at], p_send.at[h, i], p_recv.at[h, i], across)

    pairs = [(h, r) for h in range(2) for r in range(PIECES)]

    barrier = pltpu.get_barrier_semaphore()
    for dz in range(4):
        for dc in range(4):
            if dz or dc:
                to = (g, lax.rem(m + dz, 4), lax.rem(s + dc // 2, 2), lax.rem(u + dc % 2, 2))
                pl.semaphore_signal(barrier, inc=1, device_id=to, device_id_type=MESH)

    t_local = pltpu.make_async_copy(t_in, t_own, t_sems.at[2])
    v_local = pltpu.make_async_copy(v_in, v_all.at[j], t_sems.at[3])

    @pl.when(is_a)
    def _():
        for h, r in pairs:
            pltpu.make_async_copy(mine(h, r), held(2 * j + h, r), c_recv.at[2 * j + h, r]).start()

    t_local.start()
    v_local.start()
    pl.semaphore_wait(barrier, 15)

    @pl.when(is_far)
    def _():
        for h, r in pairs:
            own_far(h, r).start()

    @pl.when(is_a & (z == 1))
    def _():
        for r in range(PIECES):
            own_up(0, r).start()
            own_down(0, r).start()

    @pl.when(is_b)
    def _():
        for h, r in pairs:
            own_pair(h, r).start()

    t_copy().start()

    @pl.when(z != 1)
    def _():
        v_across(0).start()

    v_pair().start()

    odd = row == 1
    up_fa = (jnp.logical_not(odd) & (z <= 2)) | (odd & (z == 2))
    up_fb = jnp.logical_not(odd) & ((z == 1) | (z == 2))
    up_ab = (jnp.logical_not(odd) & (z == 1)) | (z == 2)
    down_fa = odd & ((z == 1) | (z == 2))
    down_fb = (odd & (z >= 1)) | (jnp.logical_not(odd) & (z == 1))
    never = z < 0

    def arrive(k, r, up, down):
        got(k, r)
        if up is not None:

            @pl.when(up)
            def _():
                z_copy(k, r, up_send, above).start()

        if down is not None:

            @pl.when(down)
            def _():
                z_copy(k, r, down_send, below).start()

    def slot_far(h, up, down):
        for r in range(PIECES):
            arrive(2 * q + h, r, up, down)
            arrive(2 * o + h, r, up, down)
        pair_copy(h, 2 * q + h).start()

    def slot_near(quarter, h):
        for r in range(PIECES):
            arrive(2 * quarter + h, r, up_ab, None)

    def adjoint(h, k, i, put):
        @pl.loop(0, following // TILE)
        def _(n):
            at = pl.ds(pl.multiple_of(n * TILE, TILE), TILE)
            put(
                n,
                at,
                lax.dot_general(
                    t_own[:, at], c_all[k], (((0,), (0,)), ((), ())),
                    preferred_element_type=jnp.float32,
                )
                + lax.dot_general(
                    t_pair[:, at], c_pair[i], (((0,), (0,)), ((), ())),
                    preferred_element_type=jnp.float32,
                ),
            )

    def partial(h):
        pair_copy(h, 2 * q + h).wait_recv()

        def put(n, at, value):
            p_out[h, at, :] = value
            p_copy(h, n).start()

        adjoint(h, 2 * o + h, h, put)

    def own_adjoint(h):
        pair_copy(2 + h, 2 * p + h).wait_recv()

        def put(n, at, value):
            adj[at, pl.ds(h * half, half)] = value

        adjoint(h, 2 * j + h, 2 + h, put)

    def gradient(parts, first=False):
        @pl.loop(0, states // TILE)
        def _(n):
            at = pl.ds(pl.multiple_of(n * TILE, TILE), TILE)
            total = None if first else grad[at, :]
            for quarter, h in parts:
                term = lax.dot_general(
                    c_all[2 * quarter + h, at, :], v_all[quarter, :, pl.ds(h * half, half)],
                    (((1,), (1,)), ((), ())), preferred_element_type=jnp.float32,
                )
                total = term if total is None else total + term
            grad[at, :] = total

    @pl.when(odd)
    def _():
        slot_near(j, 0)

    @pl.when(is_b & (z == 0))
    def _():
        for h, r in pairs:
            own_up(h, r).start()

    slot_far(0, up_fa, down_fa)

    @pl.when(is_a & (z == 0))
    def _():
        for h, r in pairs:
            own_up(h, r).start()

    @pl.when(z == 1)
    def _():
        v_across(0).start()

    v_across(1).start()
    t_local.wait()
    v_local.wait()
    t_copy().wait_recv()

    @pl.when(z >= 2)
    def _():
        partial(0)

    slot_far(1, up_fb, down_fb)

    @pl.when(is_a & (z == 1))
    def _():
        for r in range(PIECES):
            own_up(1, r).start()
            own_down(1, r).start()

    @pl.when(is_b & (z == 1))
    def _():
        for h, r in pairs:
            own_up(h, r).start()
            own_down(h, r).start()

    @pl.when(z < 2)
    def _():
        partial(0)

    @pl.when(z == 3)
    def _():
        partial(1)

    slot_near(p, 0)
    pair_copy(2, 2 * p).start()

    @pl.when(z < 3)
    def _():
        partial(1)

    for i in range(2):
        v_across(i).wait_recv()
    v_relay().start()
    gradient([(o, 0), (o, 1)], first=True)
    slot_near(p, 1)
    pair_copy(3, 2 * p + 1).start()
    v_relay().wait_recv()
    v_pair().wait_recv()
    gradient([(q, 0), (q, 1)])

    @pl.when(jnp.logical_not(odd))
    def _():
        slot_near(j, 0)

    own_adjoint(0)
    gradient([(p, 0), (p, 1), (j, 0)])
    slot_near(j, 1)
    own_adjoint(1)
    gradient([(j, 1)])
    for h in range(2):

        @pl.loop(0, following // TILE)
        def _(n):
            at = pl.ds(pl.multiple_of(n * TILE, TILE), TILE)
            p_copy(h, n).wait_recv()
            adj[at, pl.ds(h * half, half)] += p_in[h, at, :]

    for h, r in pairs:

        @pl.when(is_far)
        def _():
            own_far(h, r).wait_send()

        @pl.when(z <= 1)
        def _():
            own_up(h, r).wait_send()

        @pl.when(z == 1)
        def _():
            own_down(h, r).wait_send()

        @pl.when(is_b)
        def _():
            own_pair(h, r).wait_send()

        for k, up, down in (
            (2 * q + h, (up_fa, up_fb)[h], (down_fa, down_fb)[h]),
            (2 * o + h, (up_fa, up_fb)[h], (down_fa, down_fb)[h]),
            (2 * p + h, up_ab, None),
            (2 * j + h, up_ab, None),
        ):

            @pl.when(up)
            def _():
                z_copy(k, r, up_send, above).wait_send()

            if down is not None:

                @pl.when(down)
                def _():
                    z_copy(k, r, down_send, below).wait_send()

    for i, k in enumerate((2 * q, 2 * q + 1, 2 * p, 2 * p + 1)):
        pair_copy(i, k).wait_send()
    for i in range(2):
        v_across(i).wait_send()
    v_relay().wait_send()
    v_pair().wait_send()
    t_copy().wait_send()
    for h in range(2):
        for n in range(following // TILE):
            p_copy(h, n).wait_send()


def exchanged(expected_cot, value_next, transition, section):
    states, cells = expected_cot.shape
    current, following = transition.shape
    dma = pltpu.SemaphoreType.DMA
    half = cells // 2
    tiles = following // TILE
    adjoint_sum, gradient_sum = pl.pallas_call(
        kernel,
        out_shape=(
            jax.ShapeDtypeStruct((following, cells), jnp.float32),
            jax.ShapeDtypeStruct((current, following), jnp.float32),
        ),
        in_specs=[pl.BlockSpec(memory_space=pltpu.HBM)] * 3,
        out_specs=(pl.BlockSpec(memory_space=pltpu.VMEM),) * 2,
        scratch_shapes=[
            pltpu.VMEM((8, states, half), jnp.bfloat16),
            pltpu.VMEM((4, states, half), jnp.bfloat16),
            pltpu.VMEM((current, following), jnp.bfloat16),
            pltpu.VMEM((current, following), jnp.bfloat16),
            pltpu.VMEM((4, states, cells), jnp.bfloat16),
            pltpu.VMEM((2, following, half), jnp.float32),
            pltpu.VMEM((2, following, half), jnp.float32),
            dma((8, PIECES)),
            dma((8, PIECES)),
            dma((8, PIECES)),
            dma((2, PIECES)),
            dma((4, PIECES)),
            dma((4,)),
            dma((4,)),
            dma((4,)),
            dma((4,)),
            dma((4,)),
            dma((2, tiles)),
            dma((2, tiles)),
        ],
        compiler_params=pltpu.CompilerParams(
            collective_id=0, has_side_effects=True, vmem_limit_bytes=VMEM_BYTES
        ),
    )(*(pltpu.with_memory_space_constraint(x, pltpu.HBM) for x in (expected_cot, value_next, transition)))
    discount_factor = discount_of(section)
    return (discount_factor * adjoint_sum, discount_factor * gradient_sum)


def solution(mesh):
    shape = mesh.shape
    paired = shape["storage"] == 2 and shape["sub"] == 2 and shape["markov"] == 4
    body = exchanged if paired else gathered
    return jax.shard_map(
        body,
        mesh=mesh,
        in_specs=(
            P(("groups", "markov"), ("storage", "sub")),
            P(("groups", "markov"), ("storage", "sub")),
            P(("groups", "storage", "sub"), "markov"),
            P("groups"),
        ),
        out_specs=(
            P(("groups", "markov"), ("storage", "sub")),
            P(("groups", "storage", "sub"), "markov"),
        ),
        check_vma=False,
    )
```

```python
import jax
import jax.numpy as jnp
from jax import lax
from jax.experimental import pallas as pl
from jax.experimental.pallas import tpu as pltpu
from jax.sharding import PartitionSpec as P

discount_rate = 0.97
MESH = pl.DeviceIdType.MESH
PIECES = 4
TILE = 256
MESSAGE = TILE + TILE // 2 + 16
VMEM_BYTES = 40 * 1024 * 1024

PLAN = (
    ('v', 1, (0, 1)),
    ('own', 'd0', (2,)),
    ('own', 'u0', (3,)),
    ('own', 'f0', (4, 5, 6, 7)),
    ('wait', (2, 2, -1, -1, -1, -1, -1, -1)),
    ('pair', 2, (0, 1)),
    ('v', 1, (2, 4)),
    ('own', 'u1', (3,)),
    ('v', 0, (6, 7)),
    ('wait', (3, -1, -1, -1, -1, -1, -1, -1)),
    ('pair', 3, (0,)),
    ('v', 0, (1,)),
    ('wait', (-1, -1, -1, 2, -1, -1, -1, -1)),
    ('pair', 2, (3,)),
    ('own', 'f1', (4, 6)),
    ('own', 'u0', (1,)),
    ('wait', (-1, -1, -1, 3, -1, -1, -1, -1)),
    ('pair', 3, (3,)),
    ('v', 0, (4,)),
    ('v', 1, (6,)),
    ('v', 1, (3,)),
    ('v', 0, (3,)),
    ('hop', (66, -1, 66, 97, 66, 2, -1, 96)),
    ('v', 0, (2,)),
    ('v', 1, (5,)),
    ('hop', (98, -1, 98, 65, 98, 6, -1, 64)),
    ('hop', (70, -1, 70, 101, 70, 99, -1, 105)),
    ('hop', (102, -1, 102, 69, 102, 67, -1, 100)),
    ('hop', (74, -1, 74, 105, 74, 10, -1, 68)),
    ('hop', (106, -1, 106, 73, 106, 14, -1, 73)),
    ('v', 0, (0,)),
    ('own', 'f1', (7,)),
    ('v', 1, (7,)),
    ('hop', (78, -1, 78, -1, 78, 103, -1, 109)),
    ('own', 'u1', (2,)),
    ('pair', 0, (7,)),
    ('hop', (110, -1, 110, -1, 110, 71, -1, 77)),
    ('pair', 0, (0, 2, 4)),
    ('hop', (-1, -1, 115, -1, 114, 18, -1, 81)),
    ('own', 'f1', (5,)),
    ('v', 0, (5,)),
    ('hop', (-1, -1, 83, -1, -1, 22, -1, 85)),
    ('hop', (-1, -1, 119, -1, -1, 26, -1, 89)),
    ('hop', (-1, -1, -1, -1, -1, 30, -1, -1)),
    ('hop', (-1, -1, -1, -1, -1, 105, -1, -1)),
    ('hop', (-1, -1, -1, -1, -1, 73, -1, -1)),
    ('hop', (-1, -1, -1, -1, -1, 50, -1, -1)),
    ('hop', (-1, -1, -1, -1, -1, 54, -1, -1)),
    ('hop', (-1, -1, -1, -1, -1, 58, -1, -1)),
    ('hop', (-1, -1, -1, -1, -1, 62, -1, -1)),
    ('pair', 3, (5,)),
    ('hop', (-1, -1, -1, -1, -1, 109, -1, -1)),
    ('pair', 0, (5,)),
    ('wait', (-1, -1, -1, -1, -1, -1, 4, -1)),
    ('part', (-1, -1, -1, -1, -1, -1, 0, -1)),
    ('own', 'u1', (1,)),
    ('wait', (-1, -1, -1, -1, -1, -1, 6, -1)),
    ('pair', 0, (6,)),
    ('hop', (-1, -1, 87, -1, 82, 77, -1, 93)),
    ('hop', (-1, -1, 123, -1, 118, -1, -1, -1)),
    ('relay',),
    ('hop', (-1, -1, -1, -1, -1, 81, -1, 113)),
    ('part', (-1, -1, -1, -1, 0, 0, -1, -1)),
    ('wait', (0, -1, -1, 0, -1, -1, -1, 0)),
    ('grad', (0, 2, 4, 0, 4, 0, 4, 0)),
    ('hop', (-1, -1, 34, 109, 86, 85, -1, 117)),
    ('pair', 0, (3,)),
    ('hop', (-1, -1, 91, 77, 122, -1, -1, -1)),
    ('hop', (-1, -1, 38, -1, -1, -1, -1, -1)),
    ('part', (-1, -1, 0, 0, -1, -1, -1, 0)),
    ('wait', (-1, 6, -1, -1, -1, -1, -1, -1)),
    ('pair', 0, (1,)),
    ('hop', (-1, -1, 127, 81, 34, 89, -1, 121)),
    ('pair', 1, (2,)),
    ('wait', (-1, -1, -1, -1, -1, -1, -1, 3)),
    ('pair', 3, (7,)),
    ('hop', (-1, -1, 42, 85, 90, 93, -1, 125)),
    ('own', 'u0', (2,)),
    ('pair', 1, (7,)),
    ('hop', (-1, -1, 46, 89, -1, 113, -1, -1)),
    ('pair', 2, (2,)),
    ('hop', (-1, -1, 50, -1, -1, -1, -1, -1)),
    ('wait', (1, -1, -1, 1, -1, -1, -1, -1)),
    ('v_q', (1, 2, 4, 6, 7)),
    ('grad', (1, 6, 6, 1, 6, 1, 6, 6)),
    ('own', 'u0', (0,)),
    ('hop', (-1, -1, 95, 93, 38, 117, -1, -1)),
    ('hop', (-1, -1, 54, -1, 126, -1, -1, -1)),
    ('pair', 1, (4,)),
    ('wait', (-1, 4, -1, -1, -1, -1, -1, -1)),
    ('part', (0, 0, -1, 1, -1, -1, -1, -1)),
    ('own', 'u1', (0,)),
    ('hop', (-1, -1, 58, 113, 42, 121, -1, -1)),
    ('hop', (-1, -1, 62, 117, -1, 125, -1, -1)),
    ('pair', 3, (2,)),
    ('pair', 1, (5,)),
    ('hop', (-1, -1, -1, -1, -1, 34, -1, -1)),
    ('part', (-1, -1, -1, -1, -1, 1, -1, -1)),
    ('hop', (-1, -1, 2, 121, -1, -1, -1, -1)),
    ('grad', (2, 4, 2, 2, 7, 3, -1, 4)),
    ('wait', (7, -1, -1, -1, -1, -1, 7, -1)),
    ('pair', 1, (0, 6)),
    ('hop', (-1, -1, 6, 125, 46, 38, -1, -1)),
    ('own', 'd1', (2,)),
    ('pair', 1, (3,)),
    ('pair', 2, (4,)),
    ('own', 'd1', (3,)),
    ('hop', (-1, -1, 10, -1, -1, 42, -1, -1)),
    ('hop', (-1, -1, 14, -1, -1, 46, -1, -1)),
    ('pair', 2, (5,)),
    ('part', (-1, -1, 1, -1, -1, -1, -1, -1)),
    ('wait', (-1, -1, -1, -1, -1, -1, -1, 1)),
    ('v_q', (5,)),
    ('grad', (3, -1, 7, 3, 2, 6, 7, 1)),
    ('hop', (-1, -1, 18, -1, 50, -1, -1, -1)),
    ('hop', (-1, -1, 22, -1, 94, -1, -1, -1)),
    ('wait', (-1, 5, -1, -1, -1, -1, -1, -1)),
    ('part', (-1, 1, -1, -1, 1, -1, -1, 1)),
    ('own', 'd0', (3,)),
    ('wait', (-1, -1, -1, -1, -1, -1, 2, -1)),
    ('pair', 2, (6,)),
    ('hop', (-1, -1, 26, -1, 54, -1, -1, -1)),
    ('hop', (-1, -1, 30, -1, -1, -1, -1, -1)),
    ('v_q', (3,)),
    ('grad', (4, 5, 5, 6, 5, 4, -1, 5)),
    ('wait', (-1, -1, -1, -1, -1, -1, -1, 2)),
    ('pair', 2, (7,)),
    ('hop', (-1, -1, -1, -1, 58, -1, -1, -1)),
    ('hop', (-1, -1, -1, -1, 62, -1, -1, -1)),
    ('pair', 3, (4,)),
    ('hop', (-1, -1, -1, -1, 2, -1, -1, -1)),
    ('hop', (-1, -1, -1, -1, 6, -1, -1, -1)),
    ('wait', (-1, -1, -1, -1, -1, -1, 5, -1)),
    ('part', (-1, -1, -1, -1, -1, -1, 1, -1)),
    ('v_q', (0,)),
    ('grad', (6, -1, 3, 4, 3, 5, 2, 3)),
    ('wait', (-1, 3, -1, -1, -1, -1, 3, -1)),
    ('pair', 3, (1, 6)),
    ('wait', (-1, 7, -1, -1, -1, -1, -1, -1)),
    ('pair', 1, (1,)),
    ('hop', (-1, -1, -1, -1, 10, -1, -1, -1)),
    ('hop', (-1, -1, -1, -1, 14, -1, -1, -1)),
    ('hop', (-1, -1, -1, -1, 18, -1, -1, -1)),
    ('grad', (7, 3, 0, 5, 0, 7, 5, 7)),
    ('hop', (-1, -1, -1, -1, 22, -1, -1, -1)),
    ('wait', (5, -1, -1, -1, -1, -1, -1, -1)),
    ('part', (1, -1, -1, -1, -1, -1, -1, -1)),
    ('hop', (-1, -1, -1, -1, 26, -1, -1, -1)),
    ('hop', (-1, -1, -1, -1, 30, -1, -1, -1)),
    ('grad', (5, 7, 1, 7, 1, 2, 3, 2)),
    ('wait', (-1, 1, -1, -1, -1, -1, 0, -1)),
    ('adj', (0, 1, 0, 0, 0, 0, 0, 0)),
    ('grad', (-1, 1, -1, -1, -1, -1, 0, -1)),
    ('wait', (-1, 0, -1, -1, -1, -1, 1, -1)),
    ('grad', (-1, 0, -1, -1, -1, -1, 1, -1)),
    ('adj', (1, 0, 1, 1, 1, 1, 1, 1)),
)
CROSSING = (((0, 0, 0, 0), (1, 1, 1, 1)), ((2, 2, 3, 3), (3, 3, 3, 3)))


def discount_of(section):
    return jnp.exp(section[0].astype(jnp.float32) * jnp.log(jnp.float32(discount_rate)))


def gathered(expected_cot, value_next, transition, section):
    discount_factor = discount_of(section)
    cotangent_all = lax.all_gather(expected_cot, "markov", axis=0, tiled=True)
    adjoint_sum = lax.dot_general(
        lax.all_gather(transition, ("storage", "sub"), axis=0, tiled=True),
        cotangent_all,
        (((0,), (0,)), ((), ())),
        preferred_element_type=jnp.float32,
    )
    own_states = lax.all_to_all(
        cotangent_all, ("storage", "sub"), split_axis=0, concat_axis=1, tiled=True
    )
    gathered_values = lax.all_gather(value_next, ("storage", "sub"), axis=1, tiled=True)
    gradient_sum = lax.dot_general(
        own_states, gathered_values, (((1,), (1,)), ((), ())), preferred_element_type=jnp.float32
    )
    return (discount_factor * adjoint_sum, discount_factor * gradient_sum)


def pick(place, table):
    if len(set(table)) == 1:
        return table[0]
    value = table[0]
    for i, entry in enumerate(table[1:], 1):
        if entry != table[0]:
            value = jnp.where(place == i, entry, value)
    return value


def where(place, places, body):
    if len(places) == 8:
        body()
        return
    among = place == places[0]
    for i in places[1:]:
        among = among | (place == i)
    pl.when(among)(body)


def filled(table):
    return tuple(i for i, entry in enumerate(table) if entry >= 0)


def coded(value, out):
    top = jnp.maximum(jnp.max(jnp.abs(value), axis=0, keepdims=True), 2.0**-100)
    power = jnp.clip(jnp.ceil(jnp.log2(top * 1.0001)), -100, 100)
    whole = jnp.round(value * jnp.exp2(23.0 - power)).astype(jnp.int32)
    low = whole & 255
    out[:TILE, :] = ((whole - low) >> 8).astype(jnp.int16)
    n = TILE // 2
    out[TILE : TILE + n, :] = (low[:n] + 256 * low[n:] - 32768).astype(jnp.int16)
    out[TILE + n :, :] = jnp.broadcast_to(power.astype(jnp.int32), (16, value.shape[1])).astype(jnp.int16)


def decoded(message):
    n = TILE // 2
    high = message[:TILE, :].astype(jnp.int32) * 256
    low = message[TILE : TILE + n, :].astype(jnp.int32) + 32768
    power = message[TILE + n :, :].astype(jnp.int32)[:1].astype(jnp.float32)
    unit = jnp.exp2(power - 23.0)
    first = (high[:n] + (low & 255)).astype(jnp.float32) * unit
    second = (high[n:] + (low >> 8)).astype(jnp.float32) * unit
    return first, second


def kernel(
    c_in, v_in, t_in, adj, grad, c_all, c_pair, t_own, t_pair, v_all, p_out, p_in,
    c_recv, up_send, down_send, own_send, own_extra, pair_send, pair_recv,
    v_send, v_recv, t_sems, p_send, p_recv,
):
    g, m = lax.axis_index("groups"), lax.axis_index("markov")
    s, u = lax.axis_index("storage"), lax.axis_index("sub")
    far = 1 - s
    j, p, o, q = 2 * s + u, 2 * s + 1 - u, 2 * far + u, 2 * far + 1 - u
    step = 1 - 2 * s
    z = m + s * (3 - 2 * m)
    row = u + s * (1 - 2 * u)
    place = 2 * z + row
    partner, across = (g, m, s, 1 - u), (g, m, far, u)
    home = lax.rem(m, 2)

    def column(to, side, core):
        return (g, jnp.clip(to, 0, 3), side, core)

    above, below = column(m + step, s, u), column(m - step, s, u)
    up_home, down_home = column(m + step, s, home), column(m - step, s, home)
    states, half = c_all.shape[1:]
    tall = states // PIECES
    following = grad.shape[1]
    is_a, is_b = (z <= 1) & (row == z), (z <= 1) & (row != z)
    pairs = [(h, r) for h in range(2) for r in range(PIECES)]

    def remote(src, dst, send, recv, to):
        return pltpu.make_async_remote_copy(
            src_ref=src, dst_ref=dst, send_sem=send, recv_sem=recv, device_id=to, device_id_type=MESH
        )

    def quarter(c):
        if isinstance(c, int):
            return (j, p, o, q)[c]
        return jnp.where(c == 0, j, jnp.where(c == 1, p, jnp.where(c == 2, o, q)))

    def chunk(code):
        return 2 * quarter(code // 2) + code % 2

    def held(k, r):
        return c_all.at[k, pl.ds(pl.multiple_of(r * tall, tall), tall)]

    def mine(h, r):
        return c_in.at[pl.ds(r * tall, tall), pl.ds(h * half, half)]

    def got(k, r):
        remote(held(k, r), held(k, r), c_recv.at[k, r], c_recv.at[k, r], partner).wait_recv()

    def z_copy(k, r, send, to):
        return remote(held(k, r), held(k, r), send.at[k, r], c_recv.at[k, r], to)

    def own_copy(h, r, send, to):
        return remote(mine(h, r), held(2 * j + h, r), send, c_recv.at[2 * j + h, r], to)

    def own_up(h, r):
        return own_copy(h, r, own_send.at[h, r], up_home)

    def own_down(h, r):
        return own_copy(h, r, own_extra.at[h, r], down_home)

    def own_far(h, r):
        at = jnp.where(z == 3, CROSSING[0][h][r], CROSSING[1][h][r])
        return own_copy(h, r, own_send.at[h, r], column(m + step * (3 - z - at), far, home))

    def own_pair(h, r):
        return own_copy(h, r, own_extra.at[2 + h, r], partner)

    def pair_copy(i):
        k = (2 * q, 2 * q + 1, 2 * p, 2 * p + 1)[i]
        return remote(c_all.at[k], c_pair.at[i], pair_send.at[i], pair_recv.at[i], partner)

    def pair_got(i):
        remote(c_pair.at[i], c_pair.at[i], pair_recv.at[i], pair_recv.at[i], partner).wait_recv()

    def v_half(h):
        return v_in.at[:, pl.ds(h * half, half)]

    def v_across(h):
        return remote(v_half(h), v_all.at[2 * j + h], v_send.at[h], v_recv.at[h], across)

    def v_relay():
        part = v_all.at[pl.ds(2 * o, 2)]
        return remote(part, part, v_send.at[2], v_recv.at[2], partner)

    def v_pair(h):
        return remote(v_half(h), v_all.at[2 * j + h], v_send.at[3 + h], v_recv.at[3 + h], partner)

    def t_copy():
        return remote(t_in, t_pair, t_sems.at[0], t_sems.at[1], partner)

    def p_copy(h, n):
        return remote(p_out.at[h, n], p_in.at[h, n], p_send.at[h, n], p_recv.at[h, n], across)

    barrier = pltpu.get_barrier_semaphore()
    for dz in range(4):
        for dc in range(4):
            if dz or dc:
                to = (g, lax.rem(m + dz, 4), lax.rem(s + dc // 2, 2), lax.rem(u + dc % 2, 2))
                pl.semaphore_signal(barrier, inc=1, device_id=to, device_id_type=MESH)

    locals_ = [pltpu.make_async_copy(t_in, t_own, t_sems.at[2])]
    for h in range(2):
        locals_.append(pltpu.make_async_copy(v_half(h), v_all.at[2 * j + h], t_sems.at[3 + h]))

    @pl.when(is_a)
    def _():
        for h, r in pairs:
            pltpu.make_async_copy(mine(h, r), held(2 * j + h, r), c_recv.at[2 * j + h, r]).start()

    for copy in locals_:
        copy.start()
    pl.semaphore_wait(barrier, 15)

    def hop(table):
        def body():
            code = pick(place, tuple(entry // 4 for entry in table))
            k, r = chunk(code // PIECES), code % PIECES
            got(k, r)
            ups = tuple(i for i in filled(table) if table[i] % 4 >= 2)
            downs = tuple(i for i in filled(table) if table[i] % 2)
            if ups:
                where(place, ups, lambda: z_copy(k, r, up_send, above).start())
            if downs:
                where(place, downs, lambda: z_copy(k, r, down_send, below).start())

        where(place, filled(table), body)

    def bulk(table):
        def body():
            k = chunk(pick(place, table))
            for r in range(PIECES):
                got(k, r)

        where(place, filled(table), body)

    def own(name, places):
        copy, h = {"u": own_up, "d": own_down, "f": own_far}[name[0]], int(name[1])

        def body():
            for r in range(PIECES):
                copy(h, r).start()

        where(place, places, body)

    def both(t_block, at, c_block):
        return lax.dot_general(
            t_block[:, at], c_block[...], (((0,), (0,)), ((), ())), preferred_element_type=jnp.float32
        )

    def part(table):
        def body():
            h = pick(place, table)
            pair_got(h)

            @pl.loop(0, following // TILE)
            def _(n):
                at = pl.ds(pl.multiple_of(n * TILE, TILE), TILE)
                value = both(t_own, at, c_all.at[2 * o + h]) + both(t_pair, at, c_pair.at[h])
                coded(value, p_out.at[h, n])
                p_copy(h, n).start()

        where(place, filled(table), body)

    def adjoint(table):
        def body():
            h = pick(place, table)
            pair_got(2 + h)
            cut = pl.ds(pl.multiple_of(h * half, half), half)

            @pl.loop(0, following // TILE)
            def _(n):
                at = pl.ds(pl.multiple_of(n * TILE, TILE), TILE)
                value = both(t_own, at, c_all.at[2 * j + h]) + both(t_pair, at, c_pair.at[2 + h])
                p_copy(h, n).wait_recv()
                top = TILE // 2
                first, second = decoded(p_in.at[h, n])
                adj[pl.ds(pl.multiple_of(n * TILE, TILE), top), cut] = value[:top] + first
                adj[pl.ds(pl.multiple_of(n * TILE + top, top), top), cut] = value[top:] + second

        where(place, filled(table), body)

    def gradient(table, first):
        def body():
            k = chunk(pick(place, table))

            @pl.loop(0, states // TILE)
            def _(n):
                at = pl.ds(pl.multiple_of(n * TILE, TILE), TILE)
                term = lax.dot_general(
                    c_all[k, at, :], v_all[k], (((1,), (1,)), ((), ())),
                    preferred_element_type=jnp.float32,
                )
                grad[at, :] = term if first else grad[at, :] + term

        where(place, filled(table), body)

    @pl.when(is_b)
    def _():
        for h, r in pairs:
            own_pair(h, r).start()

    t_copy().start()
    for h in range(2):
        v_pair(h).start()
    ready, graded = False, False
    for kind, *rest in PLAN:
        if kind in ("part", "grad") and not ready:
            ready = True
            for copy in locals_:
                copy.wait()
            t_copy().wait_recv()
            for h in range(2):
                v_pair(h).wait_recv()
        if kind == "hop":
            hop(*rest)
        elif kind == "wait":
            bulk(*rest)
        elif kind == "own":
            own(*rest)
        elif kind == "v":
            where(place, rest[1], lambda: v_across(rest[0]).start())
        elif kind == "pair":
            where(place, rest[1], lambda: pair_copy(rest[0]).start())
        elif kind == "part":
            part(*rest)
        elif kind == "relay":
            for h in range(2):
                v_across(h).wait_recv()
            v_relay().start()
        elif kind == "v_q":
            where(place, rest[0], lambda: v_relay().wait_recv())
        elif kind == "grad":
            gradient(*rest, not graded)
            graded = True
        else:
            adjoint(*rest)

    for h, r in pairs:
        own_up(h, r).wait_send()

        @pl.when((z == 1))
        def _():
            own_down(h, r).wait_send()

        @pl.when(is_b)
        def _():
            own_pair(h, r).wait_send()

    ups, downs = {}, {}
    for kind, *rest in PLAN:
        if kind == "hop":
            for i, entry in enumerate(rest[0]):
                if entry >= 0 and entry % 4 >= 2:
                    ups.setdefault(entry // 4, []).append(i)
                if entry >= 0 and entry % 2:
                    downs.setdefault(entry // 4, []).append(i)
    for sent, send in ((ups, up_send), (downs, down_send)):
        for code in sorted(sent):
            k, r = chunk(code // PIECES), code % PIECES
            where(place, sent[code], lambda: z_copy(k, r, send, above).wait_send())
    for i in range(4):
        pair_copy(i).wait_send()
    for h in range(2):
        v_across(h).wait_send()
        v_pair(h).wait_send()
    v_relay().wait_send()
    t_copy().wait_send()
    for h in range(2):
        for n in range(following // TILE):
            p_copy(h, n).wait_send()


def exchanged(expected_cot, value_next, transition, section):
    states, cells = expected_cot.shape
    current, following = transition.shape
    dma = pltpu.SemaphoreType.DMA
    half = cells // 2
    tiles = following // TILE
    adjoint_sum, gradient_sum = pl.pallas_call(
        kernel,
        out_shape=(
            jax.ShapeDtypeStruct((following, cells), jnp.float32),
            jax.ShapeDtypeStruct((current, following), jnp.float32),
        ),
        in_specs=[pl.BlockSpec(memory_space=pltpu.HBM)] * 3,
        out_specs=(pl.BlockSpec(memory_space=pltpu.VMEM),) * 2,
        scratch_shapes=[
            pltpu.VMEM((8, states, half), jnp.bfloat16),
            pltpu.VMEM((4, states, half), jnp.bfloat16),
            pltpu.VMEM((current, following), jnp.bfloat16),
            pltpu.VMEM((current, following), jnp.bfloat16),
            pltpu.VMEM((8, states, half), jnp.bfloat16),
            pltpu.VMEM((2, tiles, MESSAGE, half), jnp.int16),
            pltpu.VMEM((2, tiles, MESSAGE, half), jnp.int16),
            dma((8, PIECES)),
            dma((8, PIECES)),
            dma((8, PIECES)),
            dma((2, PIECES)),
            dma((4, PIECES)),
            dma((4,)),
            dma((4,)),
            dma((5,)),
            dma((5,)),
            dma((5,)),
            dma((2, tiles)),
            dma((2, tiles)),
        ],
        compiler_params=pltpu.CompilerParams(
            collective_id=0, has_side_effects=True, vmem_limit_bytes=VMEM_BYTES
        ),
    )(*(pltpu.with_memory_space_constraint(x, pltpu.HBM) for x in (expected_cot, value_next, transition)))
    discount_factor = discount_of(section)
    return (discount_factor * adjoint_sum, discount_factor * gradient_sum)


def solution(mesh):
    shape = mesh.shape
    paired = shape["storage"] == 2 and shape["sub"] == 2 and shape["markov"] == 4
    body = exchanged if paired else gathered
    return jax.shard_map(
        body,
        mesh=mesh,
        in_specs=(
            P(("groups", "markov"), ("storage", "sub")),
            P(("groups", "markov"), ("storage", "sub")),
            P(("groups", "storage", "sub"), "markov"),
            P("groups"),
        ),
        out_specs=(
            P(("groups", "markov"), ("storage", "sub")),
            P(("groups", "storage", "sub"), "markov"),
        ),
        check_vma=False,
    )
```

```python
import jax
import jax.numpy as jnp
from jax import lax
from jax.experimental import pallas as pl
from jax.experimental.pallas import tpu as pltpu
from jax.sharding import PartitionSpec as P

discount_rate = 0.97
MESH = pl.DeviceIdType.MESH
PIECES = 4
TILE = 256
TALL = 512
STREAMS = 2
AHEAD = 2
MESSAGE = TILE + TILE // 2 + 16
VMEM_BYTES = 40 * 1024 * 1024

PLAN = (
    ('wait', (2, -1, -1, -1, -1, -1, -1, -1)),
    ('pair', 2, (0,)),
    ('v', 0, (1,)),
    ('own', 'u0', (2,)),
    ('own', 'x0', (3,)),
    ('own', 'f0', (4, 5, 6, 7)),
    ('wait', (3, -1, -1, -1, -1, -1, -1, -1)),
    ('pair', 3, (0,)),
    ('own', 'u0', (1,)),
    ('own', 'u1', (2,)),
    ('v', 0, (3, 4, 5)),
    ('own', 'f1', (6, 7)),
    ('own', 'u1', (1,)),
    ('v', 0, (2,)),
    ('v', 1, (3, 4, 6, 7)),
    ('wait', (-1, 3, -1, -1, -1, -1, -1, -1)),
    ('pair', 3, (1,)),
    ('v', 1, (2,)),
    ('wait', (-1, -1, -1, 2, -1, -1, -1, -1)),
    ('pair', 2, (3,)),
    ('v', 0, (6, 7)),
    ('own', 'd1', (2,)),
    ('wait', (-1, -1, -1, 3, -1, -1, -1, -1)),
    ('pair', 3, (3,)),
    ('hop', (66, -1, 87, 97, 86, 34, -1, 101)),
    ('own', 'f1', (4,)),
    ('hop', (98, -1, 119, 65, 118, 99, -1, 69)),
    ('v', 0, (0,)),
    ('hop', (70, -1, 66, 101, 66, 67, -1, 96)),
    ('hop', (102, -1, 95, 69, 94, 38, -1, 105)),
    ('v', 1, (5,)),
    ('hop', (74, -1, 127, 105, 126, 42, -1, 64)),
    ('hop', (106, -1, 98, 73, 98, 46, -1, 73)),
    ('pair', 2, (5,)),
    ('hop', (78, -1, 70, 109, 70, 101, -1, 109)),
    ('pair', 0, (3, 7)),
    ('hop', (110, -1, 102, 77, 102, 50, -1, 77)),
    ('pair', 0, (0,)),
    ('wait', (-1, -1, -1, -1, -1, -1, -1, 2)),
    ('pair', 2, (7,)),
    ('wait', (-1, -1, -1, -1, -1, -1, -1, 3)),
    ('pair', 3, (7,)),
    ('hop', (82, -1, 74, -1, 74, 69, -1, 81)),
    ('hop', (114, -1, 106, -1, 106, 54, -1, 85)),
    ('hop', (90, -1, 78, -1, 78, 105, -1, 89)),
    ('hop', (122, -1, 110, -1, -1, 58, -1, -1)),
    ('pair', 0, (2,)),
    ('hop', (84, -1, 82, -1, -1, 73, -1, -1)),
    ('hop', (-1, -1, 114, -1, -1, 62, -1, -1)),
    ('pair', 3, (5,)),
    ('hop', (-1, -1, 34, -1, -1, 109, -1, -1)),
    ('pair', 0, (5,)),
    ('hop', (-1, -1, 90, -1, -1, 77, -1, -1)),
    ('own', 'f1', (5,)),
    ('hop', (-1, -1, 38, -1, -1, 81, -1, -1)),
    ('hop', (-1, -1, 122, -1, -1, 85, -1, -1)),
    ('pair', 1, (2,)),
    ('hop', (-1, -1, 42, -1, -1, -1, -1, -1)),
    ('hop', (-1, -1, 46, -1, -1, -1, -1, -1)),
    ('pair', 2, (2,)),
    ('hop', (-1, -1, 50, -1, -1, -1, -1, -1)),
    ('hop', (-1, -1, 54, -1, -1, -1, -1, -1)),
    ('part', (-1, -1, 0, 0, 0, -1, -1, -1)),
    ('v', 1, (0, 1)),
    ('own', 'u0', (0,)),
    ('own', 'u1', (0,)),
    ('hop', (116, -1, 58, -1, 110, 95, -1, 113)),
    ('pair', 0, (4,)),
    ('hop', (-1, -1, 62, -1, 82, 89, -1, 117)),
    ('pair', 3, (2,)),
    ('hop', (-1, -1, -1, -1, 114, 113, -1, 121)),
    ('hop', (-1, -1, -1, -1, -1, 127, -1, 92)),
    ('relay',),
    ('hop', (-1, -1, -1, 81, 34, 117, -1, -1)),
    ('wait', (-1, -1, -1, -1, -1, -1, 4, -1)),
    ('part', (-1, -1, -1, -1, -1, 0, 0, -1)),
    ('wait', (-1, 6, -1, -1, -1, -1, 6, -1)),
    ('pair', 0, (1, 6)),
    ('hop', (92, -1, 2, 85, 90, 121, -1, 124)),
    ('pair', 1, (5, 7)),
    ('hop', (124, -1, 6, 93, 38, -1, -1, -1)),
    ('pair', 1, (0,)),
    ('hop', (-1, -1, 10, 89, 122, -1, -1, -1)),
    ('pair', 1, (4,)),
    ('hop', (-1, -1, 14, 113, 42, -1, -1, -1)),
    ('hop', (-1, -1, 18, 125, 46, -1, -1, -1)),
    ('pair', 2, (4,)),
    ('part', (-1, -1, -1, 1, 1, 1, -1, 0)),
    ('wait', (-1, 4, -1, -1, -1, -1, -1, -1)),
    ('part', (-1, 0, -1, -1, -1, -1, -1, -1)),
    ('hop', (-1, -1, 22, 117, 50, -1, -1, -1)),
    ('hop', (-1, -1, 26, 121, 54, -1, -1, -1)),
    ('pair', 1, (3,)),
    ('wait', (-1, -1, -1, -1, -1, -1, 5, -1)),
    ('part', (0, -1, -1, -1, -1, -1, 1, -1)),
    ('wait', (-1, -1, -1, -1, -1, -1, 7, -1)),
    ('pair', 1, (6,)),
    ('wait', (-1, -1, -1, -1, -1, -1, 2, -1)),
    ('pair', 2, (6,)),
    ('hop', (-1, -1, 30, -1, 58, -1, -1, -1)),
    ('hop', (-1, -1, -1, -1, 62, -1, -1, -1)),
    ('pair', 3, (4,)),
    ('hop', (-1, -1, -1, -1, 2, -1, -1, -1)),
    ('hop', (-1, -1, -1, -1, 6, -1, -1, -1)),
    ('wait', (0, -1, -1, 0, -1, -1, -1, -1)),
    ('grad', (0, 3, 4, 0, 4, 2, 4, 2)),
    ('hop', (-1, -1, -1, -1, 10, -1, -1, -1)),
    ('v_q', (1, 2, 4, 6, 7)),
    ('grad', (2, 6, 6, 2, 6, 3, 6, 6)),
    ('v_q', (5,)),
    ('grad', (3, 4, 5, 3, 5, 6, 5, 4)),
    ('hop', (-1, -1, -1, -1, 14, -1, -1, -1)),
    ('wait', (-1, 5, -1, -1, -1, -1, -1, -1)),
    ('v_q', (3,)),
    ('grad', (4, 5, 2, 6, 2, 4, 2, 3)),
    ('wait', (-1, 7, -1, -1, -1, -1, -1, -1)),
    ('pair', 1, (1,)),
    ('v_q', (0,)),
    ('grad', (6, 7, 7, 4, 7, 5, 7, 5)),
    ('own', 'u0', (3,)),
    ('wait', (-1, -1, -1, -1, -1, -1, 3, -1)),
    ('pair', 3, (6,)),
    ('hop', (-1, -1, -1, -1, 18, -1, -1, -1)),
    ('hop', (-1, -1, -1, -1, 22, -1, -1, -1)),
    ('grad', (5, -1, 3, 5, 3, 7, 3, 7)),
    ('own', 'd0', (2,)),
    ('part', (1, 1, 1, -1, -1, -1, -1, 1)),
    ('hop', (-1, -1, -1, -1, 26, 0, -1, -1)),
    ('grad', (7, -1, 0, 7, 0, -1, -1, -1)),
    ('wait', (-1, 2, -1, -1, -1, -1, -1, -1)),
    ('pair', 2, (1,)),
    ('own', 'd0', (3,)),
    ('hop', (-1, -1, -1, -1, 30, 4, -1, -1)),
    ('hop', (-1, -1, -1, -1, -1, 10, -1, -1)),
    ('hop', (-1, -1, -1, -1, -1, 14, -1, -1)),
    ('wait', (-1, -1, -1, -1, -1, -1, 0, 0)),
    ('grad', (-1, 2, -1, -1, -1, 0, 0, 0)),
    ('wait', (-1, 0, -1, -1, -1, -1, -1, -1)),
    ('adj', (0, 0, 0, 0, 0, 0, 0, 0)),
    ('own', 'u1', (3,)),
    ('own', 'd1', (3,)),
    ('hop', (-1, -1, -1, -1, -1, 18, -1, -1)),
    ('hop', (-1, -1, -1, -1, -1, 22, -1, -1)),
    ('hop', (-1, -1, -1, -1, -1, 26, -1, -1)),
    ('hop', (-1, -1, -1, -1, -1, 30, -1, -1)),
    ('grad', (-1, 0, -1, -1, -1, -1, -1, -1)),
    ('pre', (1, 1, 1, 1, 1, 1, 1, 1)),
    ('fin', (1, 1, 1, 1, 1, 1, 1, 1), (0, 1, 3, 6, 7)),
)
CROSSING = (((0, 0, 0, 0), (0, 1, 0, 1)), ((2, 3, 3, 3), (3, 3, 3, 2)))


def discount_of(section):
    return jnp.exp(section.astype(jnp.float32) * jnp.log(jnp.float32(discount_rate)))


def gathered(expected_cot, value_next, transition, section):
    discount_factor = discount_of(section[0])
    cotangent_all = lax.all_gather(expected_cot, "markov", axis=0, tiled=True)
    adjoint_sum = lax.dot_general(
        lax.all_gather(transition, ("storage", "sub"), axis=0, tiled=True),
        cotangent_all,
        (((0,), (0,)), ((), ())),
        preferred_element_type=jnp.float32,
    )
    own_states = lax.all_to_all(
        cotangent_all, ("storage", "sub"), split_axis=0, concat_axis=1, tiled=True
    )
    gathered_values = lax.all_gather(value_next, ("storage", "sub"), axis=1, tiled=True)
    gradient_sum = lax.dot_general(
        own_states, gathered_values, (((1,), (1,)), ((), ())), preferred_element_type=jnp.float32
    )
    return (discount_factor * adjoint_sum, discount_factor * gradient_sum)


def pick(place, table):
    if len(set(table)) == 1:
        return table[0]
    value = table[0]
    for i, entry in enumerate(table[1:], 1):
        if entry != table[0]:
            value = jnp.where(place == i, entry, value)
    return value


def where(place, places, body):
    if len(places) == 8:
        body()
        return
    among = place == places[0]
    for i in places[1:]:
        among = among | (place == i)
    pl.when(among)(body)


def filled(table):
    return tuple(i for i, entry in enumerate(table) if entry >= 0)


def coded(value, out):
    top = jnp.maximum(jnp.max(jnp.abs(value), axis=0, keepdims=True), 2.0**-100)
    power = jnp.clip(jnp.ceil(jnp.log2(top * 1.0001)), -100, 100)
    whole = jnp.round(value * jnp.exp2(23.0 - power)).astype(jnp.int32)
    low = whole & 255
    out[:TILE, :] = ((whole - low) >> 8).astype(jnp.int16)
    n = TILE // 2
    out[TILE : TILE + n, :] = (low[:n] + 256 * low[n:] - 32768).astype(jnp.int16)
    out[TILE + n :, :] = jnp.broadcast_to(power.astype(jnp.int32), (16, value.shape[1])).astype(jnp.int16)


def decoded(message):
    n = TILE // 2
    high = message[:TILE, :].astype(jnp.int32) * 256
    low = message[TILE : TILE + n, :].astype(jnp.int32) + 32768
    power = message[TILE + n :, :].astype(jnp.int32)[:1].astype(jnp.float32)
    unit = jnp.exp2(power - 23.0)
    first = (high[:n] + (low & 255)).astype(jnp.float32) * unit
    second = (high[n:] + (low >> 8)).astype(jnp.float32) * unit
    return first, second


def kernel(
    section, c_in, v_in, t_in, adj, grad, c_all, c_pair, t_own, t_pair, v_all, p_out, p_in,
    c_recv, up_send, down_send, own_send, own_extra, pair_send, pair_recv,
    v_send, v_recv, t_sems, p_send, p_recv,
):
    g, m = lax.axis_index("groups"), lax.axis_index("markov")
    s, u = lax.axis_index("storage"), lax.axis_index("sub")
    far = 1 - s
    j, p, o, q = 2 * s + u, 2 * s + 1 - u, 2 * far + u, 2 * far + 1 - u
    step = 1 - 2 * s
    z = m + s * (3 - 2 * m)
    row = u + s * (1 - 2 * u)
    place = 2 * z + row
    partner, across = (g, m, s, 1 - u), (g, m, far, u)
    home = lax.rem(m, 2)

    def column(to, side, core):
        return (g, jnp.clip(to, 0, 3), side, core)

    above, below = column(m + step, s, u), column(m - step, s, u)
    up_home, down_home = column(m + step, s, home), column(m - step, s, home)
    states, half = c_all.shape[1:]
    tall = states // PIECES
    following = grad.shape[1]
    is_a, is_b = (z <= 1) & (row == z), (z <= 1) & (row != z)
    pairs = [(h, r) for h in range(2) for r in range(PIECES)]

    def remote(src, dst, send, recv, to):
        return pltpu.make_async_remote_copy(
            src_ref=src, dst_ref=dst, send_sem=send, recv_sem=recv, device_id=to, device_id_type=MESH
        )

    def quarter(c):
        if isinstance(c, int):
            return (j, p, o, q)[c]
        return jnp.where(c == 0, j, jnp.where(c == 1, p, jnp.where(c == 2, o, q)))

    def chunk(code):
        return 2 * quarter(code // 2) + code % 2

    def held(k, r):
        return c_all.at[k, pl.ds(pl.multiple_of(r * tall, tall), tall)]

    def mine(h, r):
        return c_in.at[pl.ds(r * tall, tall), pl.ds(h * half, half)]

    def got(k, r):
        remote(held(k, r), held(k, r), c_recv.at[k, r], c_recv.at[k, r], partner).wait_recv()

    def z_copy(k, r, send, to):
        return remote(held(k, r), held(k, r), send.at[k, r], c_recv.at[k, r], to)

    def own_copy(h, r, send, to):
        return remote(mine(h, r), held(2 * j + h, r), send, c_recv.at[2 * j + h, r], to)

    def own_up(h, r):
        return own_copy(h, r, own_send.at[h, r], up_home)

    def own_down(h, r):
        return own_copy(h, r, own_extra.at[h, r], down_home)

    def own_far(h, r):
        at = jnp.where(z == 3, CROSSING[0][h][r], CROSSING[1][h][r])
        return own_copy(h, r, own_send.at[h, r], column(m + step * (3 - z - at), far, home))

    def own_ahead(h, r):
        return own_copy(h, r, own_extra.at[2 + h, r], column(m + 2 * step, s, home))

    def own_pair(h, r):
        return own_copy(h, r, own_extra.at[2 + h, r], partner)

    def pair_copy(i):
        k = (2 * q, 2 * q + 1, 2 * p, 2 * p + 1)[i]
        return remote(c_all.at[k], c_pair.at[i], pair_send.at[i], pair_recv.at[i], partner)

    def pair_got(i):
        remote(c_pair.at[i], c_pair.at[i], pair_recv.at[i], pair_recv.at[i], partner).wait_recv()

    def v_half(h):
        return v_in.at[:, pl.ds(h * half, half)]

    def v_across(h):
        return remote(v_half(h), v_all.at[2 * j + h], v_send.at[h], v_recv.at[h], across)

    def v_relay():
        part = v_all.at[pl.ds(2 * o, 2)]
        return remote(part, part, v_send.at[2], v_recv.at[2], partner)

    def v_pair(h):
        return remote(v_half(h), v_all.at[2 * j + h], v_send.at[3 + h], v_recv.at[3 + h], partner)

    def t_copy():
        return remote(t_in, t_pair, t_sems.at[0], t_sems.at[1], partner)

    def p_copy(h, n):
        return remote(p_out.at[h, n], p_in.at[h, n], p_send.at[h, n], p_recv.at[h, n], across)

    barrier = pltpu.get_barrier_semaphore()
    for dz in range(4):
        for dc in range(4):
            if dz or dc:
                to = (g, lax.rem(m + dz, 4), lax.rem(s + dc // 2, 2), lax.rem(u + dc % 2, 2))
                pl.semaphore_signal(barrier, inc=1, device_id=to, device_id_type=MESH)

    locals_ = [pltpu.make_async_copy(t_in, t_own, t_sems.at[2])]
    for h in range(2):
        locals_.append(pltpu.make_async_copy(v_half(h), v_all.at[2 * j + h], t_sems.at[3 + h]))

    @pl.when(is_a)
    def _():
        for h, r in pairs:
            pltpu.make_async_copy(mine(h, r), held(2 * j + h, r), c_recv.at[2 * j + h, r]).start()

    for copy in locals_:
        copy.start()
    pl.semaphore_wait(barrier, 15)

    def hop(table):
        def body():
            code = pick(place, tuple(entry // 4 for entry in table))
            k, r = chunk(code // PIECES), code % PIECES
            got(k, r)
            ups = tuple(i for i in filled(table) if table[i] % 4 >= 2)
            downs = tuple(i for i in filled(table) if table[i] % 2)
            if ups:
                where(place, ups, lambda: z_copy(k, r, up_send, above).start())
            if downs:
                where(place, downs, lambda: z_copy(k, r, down_send, below).start())

        where(place, filled(table), body)

    def bulk(table):
        def body():
            k = chunk(pick(place, table))
            for r in range(PIECES):
                got(k, r)

        where(place, filled(table), body)

    def own(name, places):
        copy, h = {"u": own_up, "d": own_down, "f": own_far, "x": own_ahead}[name[0]], int(name[1])

        def body():
            for r in range(AHEAD if name[0] == "x" else PIECES):
                copy(h, r).start()

        where(place, places, body)

    def both(t_block, at, c_block):
        return lax.dot_general(
            t_block[:, at], c_block[...], (((0,), (0,)), ((), ())), preferred_element_type=jnp.float32
        )

    def part(table):
        def body():
            h = pick(place, table)
            pair_got(h)

            @pl.loop(0, following // TILE)
            def _(n):
                at = pl.ds(pl.multiple_of(n * TILE, TILE), TILE)
                value = both(t_own, at, c_all.at[2 * o + h]) + both(t_pair, at, c_pair.at[h])
                coded(value, p_out.at[h, n])
                p_copy(h, n).start()

        where(place, filled(table), body)

    def adjoint(table, factor):
        def body():
            h = pick(place, table)
            pair_got(2 + h)
            cut = pl.ds(pl.multiple_of(h * half, half), half)

            @pl.loop(0, following // TILE)
            def _(n):
                at = pl.ds(pl.multiple_of(n * TILE, TILE), TILE)
                value = both(t_own, at, c_all.at[2 * j + h]) + both(t_pair, at, c_pair.at[2 + h])
                p_copy(h, n).wait_recv()
                top = TILE // 2
                first, second = decoded(p_in.at[h, n])
                adj[pl.ds(pl.multiple_of(n * TILE, TILE), top), cut] = factor * (value[:top] + first)
                adj[pl.ds(pl.multiple_of(n * TILE + top, top), top), cut] = factor * (value[top:] + second)

        where(place, filled(table), body)

    def product(k, at):
        return lax.dot_general(
            c_all[k, at, :], v_all[k], (((1,), (1,)), ((), ())), preferred_element_type=jnp.float32
        )

    def gradient(table, first):
        def body():
            k = chunk(pick(place, table))

            @pl.loop(0, states // TALL)
            def _(n):
                at = pl.ds(pl.multiple_of(n * TALL, TALL), TALL)
                grad[at, :] = product(k, at) if first else grad[at, :] + product(k, at)

        where(place, filled(table), body)

    tiles = following // TILE

    def cut_of(h):
        return pl.ds(pl.multiple_of(h * half, half), half)

    def add_partial(h, n, scale):
        p_copy(h, n).wait_recv()
        top = TILE // 2
        for i, value in enumerate(decoded(p_in.at[h, n])):
            at = pl.ds(n * TILE + i * top, top)
            adj[at, cut_of(h)] = scale(adj[at, cut_of(h)] + value)

    def begin(table):
        h = pick(place, table)
        pair_got(2 + h)

        @pl.loop(0, tiles)
        def _(n):
            at = pl.ds(pl.multiple_of(n * TILE, TILE), TILE)
            adj[at, cut_of(h)] = both(t_pair, at, c_pair.at[2 + h])

        for n in range(tiles - 1):
            add_partial(h, n, lambda value: value)

    def finish(table, late, factor):
        h = pick(place, table)
        k = 2 * j + h

        @pl.loop(0, PIECES)
        def _(r):
            where(place, late, lambda: got(k, r))
            at = pl.ds(pl.multiple_of(r * tall, tall), tall)
            grad[at, :] = factor * (grad[at, :] + product(k, at))
            adj[:, cut_of(h)] += lax.dot_general(
                t_own[at, :], c_all[k, at, :], (((0,), (0,)), ((), ())),
                preferred_element_type=jnp.float32,
            )

        done = pl.ds(0, (tiles - 1) * TILE)
        adj[done, cut_of(h)] = factor * adj[done, cut_of(h)]
        add_partial(h, tiles - 1, lambda value: factor * value)

    @pl.when(is_b)
    def _():
        for h, r in pairs:
            own_pair(h, r).start()

    t_copy().start()
    for h in range(2):
        v_pair(h).start()
    ready, graded = False, False
    for kind, *rest in PLAN:
        if kind in ("part", "grad") and not ready:
            ready = True
            factor = jnp.max(discount_of(jnp.full((8, 128), section[0])))
            for copy in locals_:
                copy.wait()
            t_copy().wait_recv()
            for h in range(2):
                v_pair(h).wait_recv()
        if kind == "hop":
            hop(*rest)
        elif kind == "wait":
            bulk(*rest)
        elif kind == "own":
            own(*rest)
        elif kind == "v":
            where(place, rest[1], lambda: v_across(rest[0]).start())
        elif kind == "pair":
            where(place, rest[1], lambda: pair_copy(rest[0]).start())
        elif kind == "part":
            part(*rest)
        elif kind == "relay":
            for h in range(2):
                v_across(h).wait_recv()
            v_relay().start()
        elif kind == "v_q":
            where(place, rest[0], lambda: v_relay().wait_recv())
        elif kind == "grad":
            gradient(*rest, not graded)
            graded = True
        elif kind == "adj":
            adjoint(*rest, factor)
        elif kind == "pre":
            begin(*rest)
        else:
            finish(*rest, factor)

    for h, r in pairs:
        own_up(h, r).wait_send()

        @pl.when((z == 1))
        def _():
            own_down(h, r).wait_send()

        @pl.when(is_b)
        def _():
            own_pair(h, r).wait_send()

    for r in range(AHEAD):
        pl.when(is_a & (z == 1))(lambda: own_ahead(0, r).wait_send())

    ups, downs = {}, {}
    for kind, *rest in PLAN:
        if kind == "hop":
            for i, entry in enumerate(rest[0]):
                if entry >= 0 and entry % 4 >= 2:
                    ups.setdefault(entry // 4, []).append(i)
                if entry >= 0 and entry % 2:
                    downs.setdefault(entry // 4, []).append(i)
    for sent, send in ((ups, up_send), (downs, down_send)):
        for code in sorted(sent):
            k, r = chunk(code // PIECES), code % PIECES
            where(place, sent[code], lambda: z_copy(k, r, send, above).wait_send())
    for i in range(4):
        pair_copy(i).wait_send()
    for h in range(2):
        v_across(h).wait_send()
        v_pair(h).wait_send()
    v_relay().wait_send()
    t_copy().wait_send()
    for h in range(2):
        for n in range(following // TILE):
            p_copy(h, n).wait_send()


def stored(adj, grad, adj_out, grad_out, sems):
    copies = []
    for i, (src, dst) in enumerate(((grad, grad_out), (adj, adj_out))):
        tall = src.shape[0] // STREAMS
        for n in range(STREAMS):
            at = pl.ds(n * tall, tall)
            copies.append(pltpu.make_async_copy(src.at[at], dst.at[at], sems.at[i, n]))
    for copy in copies:
        copy.start()
    for copy in copies:
        copy.wait()


def exchanged(expected_cot, value_next, transition, section):
    states, cells = expected_cot.shape
    current, following = transition.shape
    dma = pltpu.SemaphoreType.DMA
    half = cells // 2
    tiles = following // TILE
    arrays = (expected_cot, value_next, transition)
    sums = pl.pallas_call(
        kernel,
        out_shape=(
            jax.ShapeDtypeStruct((following, cells), jnp.float32),
            jax.ShapeDtypeStruct((current, following), jnp.float32),
        ),
        in_specs=[pl.BlockSpec(memory_space=pltpu.SMEM)] + [pl.BlockSpec(memory_space=pltpu.HBM)] * 3,
        out_specs=(pl.BlockSpec(memory_space=pltpu.VMEM),) * 2,
        scratch_shapes=[
            pltpu.VMEM((8, states, half), jnp.bfloat16),
            pltpu.VMEM((4, states, half), jnp.bfloat16),
            pltpu.VMEM((current, following), jnp.bfloat16),
            pltpu.VMEM((current, following), jnp.bfloat16),
            pltpu.VMEM((8, states, half), jnp.bfloat16),
            pltpu.VMEM((2, tiles, MESSAGE, half), jnp.int16),
            pltpu.VMEM((2, tiles, MESSAGE, half), jnp.int16),
            dma((8, PIECES)),
            dma((8, PIECES)),
            dma((8, PIECES)),
            dma((2, PIECES)),
            dma((4, PIECES)),
            dma((4,)),
            dma((4,)),
            dma((5,)),
            dma((5,)),
            dma((5,)),
            dma((2, tiles)),
            dma((2, tiles)),
        ],
        compiler_params=pltpu.CompilerParams(
            collective_id=0, has_side_effects=True, vmem_limit_bytes=VMEM_BYTES
        ),
    )(section, *(pltpu.with_memory_space_constraint(x, pltpu.HBM) for x in arrays))
    return pl.pallas_call(
        stored,
        out_shape=tuple(jax.ShapeDtypeStruct(x.shape, x.dtype) for x in sums),
        in_specs=[pl.BlockSpec(memory_space=pltpu.VMEM)] * 2,
        out_specs=(pl.BlockSpec(memory_space=pltpu.HBM),) * 2,
        scratch_shapes=[dma((2, STREAMS))],
        compiler_params=pltpu.CompilerParams(vmem_limit_bytes=1024 * 1024),
    )(*(pltpu.with_memory_space_constraint(x, pltpu.VMEM) for x in sums))


def solution(mesh):
    shape = mesh.shape
    paired = shape["storage"] == 2 and shape["sub"] == 2 and shape["markov"] == 4
    body = exchanged if paired else gathered
    return jax.shard_map(
        body,
        mesh=mesh,
        in_specs=(
            P(("groups", "markov"), ("storage", "sub")),
            P(("groups", "markov"), ("storage", "sub")),
            P(("groups", "storage", "sub"), "markov"),
            P("groups"),
        ),
        out_specs=(
            P(("groups", "markov"), ("storage", "sub")),
            P(("groups", "storage", "sub"), "markov"),
        ),
        check_vma=False,
    )
```

```python
import jax
import jax.numpy as jnp
from jax import lax
from jax.experimental import pallas as pl
from jax.experimental.pallas import tpu as pltpu
from jax.sharding import PartitionSpec as P

discount_rate = 0.97
MESH = pl.DeviceIdType.MESH
PIECES = 4
TILE = 256
TALL = 512
STREAMS = 2
AHEAD = 0
BITS = 20
BASE = 2 ** (BITS - 16)
SHARE = 16 // (BITS - 16)
MESSAGE = TILE + TILE // SHARE + 16
VMEM_BYTES = 40 * 1024 * 1024

PLAN = (
    ('v', 0, (0, 1)),
    ('own', 'u1', (2,)),
    ('v', 1, (3, 4, 5)),
    ('own', 'f0', (6, 7)),
    ('v', 1, (0, 1)),
    ('own', 'd1', (2,)),
    ('wait', (-1, -1, -1, 2, -1, -1, -1, -1)),
    ('pair', 2, (3,)),
    ('own', 'f0', (4, 5)),
    ('own', 'f1', (6, 7)),
    ('wait', (2, -1, -1, -1, -1, -1, -1, -1)),
    ('pair', 2, (0,)),
    ('own', 'u0', (1,)),
    ('v', 1, (2,)),
    ('wait', (-1, -1, -1, 3, -1, -1, -1, -1)),
    ('pair', 3, (3,)),
    ('own', 'f1', (4,)),
    ('v', 0, (6, 7)),
    ('wait', (3, -1, -1, -1, -1, -1, -1, -1)),
    ('pair', 3, (0,)),
    ('own', 'u1', (1,)),
    ('own', 'u0', (2,)),
    ('v', 0, (3, 4)),
    ('v', 1, (6, 7)),
    ('wait', (-1, 3, -1, -1, -1, -1, -1, -1)),
    ('pair', 3, (1,)),
    ('v', 0, (2,)),
    ('hop', (66, -1, 83, 97, 82, 50, -1, 97)),
    ('hop', (98, -1, 115, -1, 114, 54, -1, 65)),
    ('hop', (70, -1, 66, -1, 66, 58, -1, 101)),
    ('wait', (-1, -1, -1, -1, -1, -1, -1, 3)),
    ('pair', 3, (7,)),
    ('hop', (102, -1, 87, -1, 86, 62, -1, 69)),
    ('pair', 3, (5,)),
    ('own', 'f1', (5,)),
    ('hop', (74, -1, 98, -1, 98, 34, -1, 105)),
    ('v', 0, (5,)),
    ('hop', (106, -1, 119, -1, 118, 38, -1, 73)),
    ('hop', (78, -1, 70, -1, 70, 97, -1, 109)),
    ('pair', 0, (7,)),
    ('wait', (-1, -1, -1, -1, -1, -1, -1, 2)),
    ('pair', 2, (7,)),
    ('hop', (110, -1, 102, -1, 102, 42, -1, 77)),
    ('pair', 0, (0,)),
    ('hop', (90, -1, 74, -1, 74, 65, -1, 113)),
    ('hop', (122, -1, 106, -1, 106, 46, -1, 81)),
    ('pair', 2, (5,)),
    ('hop', (94, -1, 78, -1, 78, 101, -1, 117)),
    ('hop', (126, -1, 110, -1, -1, 69, -1, 85)),
    ('pair', 0, (2,)),
    ('hop', (80, -1, 90, -1, -1, 105, -1, 125)),
    ('hop', (-1, -1, 122, -1, -1, 73, -1, 120)),
    ('pair', 1, (7,)),
    ('hop', (-1, -1, 34, -1, -1, 109, -1, 93)),
    ('pair', 0, (5,)),
    ('hop', (-1, -1, 94, -1, -1, 77, -1, -1)),
    ('hop', (-1, -1, 38, -1, -1, 113, -1, -1)),
    ('hop', (-1, -1, 126, -1, -1, 81, -1, -1)),
    ('pair', 1, (2,)),
    ('hop', (-1, -1, 42, -1, -1, 123, -1, -1)),
    ('hop', (-1, -1, 46, -1, -1, 91, -1, -1)),
    ('pair', 2, (2,)),
    ('hop', (-1, -1, -1, -1, -1, 117, -1, -1)),
    ('hop', (-1, -1, -1, -1, -1, 85, -1, -1)),
    ('part', (-1, -1, -1, -1, 0, -1, -1, -1)),
    ('hop', (112, -1, 50, 65, 110, 125, -1, 88)),
    ('pair', 0, (4,)),
    ('pair', 1, (5,)),
    ('hop', (84, -1, 54, 101, 90, 93, -1, -1)),
    ('own', 'u0', (0,)),
    ('own', 'u1', (0,)),
    ('hop', (116, -1, 58, 69, 122, -1, -1, -1)),
    ('pair', 1, (0,)),
    ('hop', (-1, -1, 62, 105, 34, -1, -1, -1)),
    ('pair', 3, (2,)),
    ('hop', (-1, -1, -1, 73, 94, -1, -1, -1)),
    ('wait', (-1, -1, -1, -1, -1, -1, 4, -1)),
    ('part', (-1, -1, -1, -1, 1, 0, 0, -1)),
    ('wait', (-1, -1, -1, -1, -1, -1, 6, -1)),
    ('pair', 0, (6,)),
    ('hop', (-1, -1, -1, 109, -1, -1, -1, -1)),
    ('pair', 0, (3,)),
    ('relay',),
    ('hop', (-1, -1, -1, 77, 38, -1, -1, -1)),
    ('part', (-1, -1, -1, 0, -1, -1, -1, -1)),
    ('hop', (-1, -1, 2, 113, 126, -1, -1, -1)),
    ('pair', 1, (4,)),
    ('hop', (-1, -1, 6, 81, 42, -1, -1, -1)),
    ('hop', (-1, -1, 10, 121, 46, -1, -1, -1)),
    ('pair', 2, (4,)),
    ('wait', (-1, -1, -1, -1, -1, -1, 5, -1)),
    ('part', (-1, -1, 0, -1, -1, 1, 1, 0)),
    ('wait', (-1, 6, -1, -1, -1, -1, -1, -1)),
    ('pair', 0, (1,)),
    ('own', 'u0', (3,)),
    ('hop', (-1, -1, 14, 89, 50, -1, -1, -1)),
    ('hop', (-1, -1, 18, -1, 54, -1, -1, -1)),
    ('wait', (-1, 4, -1, -1, -1, -1, -1, -1)),
    ('part', (-1, 0, -1, -1, -1, -1, -1, -1)),
    ('wait', (-1, -1, -1, -1, -1, -1, 7, -1)),
    ('pair', 1, (6,)),
    ('wait', (-1, -1, -1, -1, -1, -1, 2, -1)),
    ('pair', 2, (6,)),
    ('hop', (-1, -1, 22, 117, 58, -1, -1, -1)),
    ('hop', (-1, -1, 26, 85, -1, -1, -1, -1)),
    ('wait', (0, -1, -1, 0, -1, -1, -1, -1)),
    ('grad', (0, 3, 4, 0, 4, 3, 4, 3)),
    ('hop', (-1, -1, -1, 125, -1, 2, -1, -1)),
    ('pair', 1, (3,)),
    ('v_q', (1, 2, 4, 6)),
    ('grad', (2, 6, 6, 2, 6, 2, 6, 2)),
    ('v_q', (5, 7)),
    ('grad', (3, 4, 5, 3, 5, 6, 5, 6)),
    ('v_q', (3,)),
    ('grad', (4, -1, 2, 6, 2, 4, 2, 4)),
    ('wait', (-1, 7, -1, -1, -1, -1, -1, -1)),
    ('pair', 1, (1,)),
    ('hop', (-1, -1, 30, 93, 62, 6, -1, -1)),
    ('pair', 3, (4,)),
    ('hop', (-1, -1, -1, -1, 2, 10, -1, -1)),
    ('hop', (-1, -1, -1, -1, 6, -1, -1, -1)),
    ('v_q', (0,)),
    ('grad', (6, 7, 7, 4, 7, 7, 7, 7)),
    ('own', 'd0', (2,)),
    ('wait', (-1, -1, -1, -1, -1, -1, 3, -1)),
    ('pair', 3, (6,)),
    ('hop', (-1, -1, -1, -1, 10, 14, -1, -1)),
    ('hop', (-1, -1, -1, -1, 14, -1, -1, -1)),
    ('wait', (-1, 5, -1, -1, -1, -1, -1, -1)),
    ('grad', (5, 5, 3, 7, 3, 5, 3, 5)),
    ('part', (0, 1, 1, 1, -1, -1, -1, 1)),
    ('part', (1, -1, -1, -1, -1, -1, -1, -1)),
    ('grad', (7, -1, 0, 5, 0, 0, -1, -1)),
    ('hop', (-1, -1, -1, -1, 18, -1, -1, -1)),
    ('adj', (-1, -1, 0, 0, 0, 0, -1, -1)),
    ('wait', (-1, 2, -1, -1, -1, -1, -1, -1)),
    ('pair', 2, (1,)),
    ('own', 'd1', (3,)),
    ('hop', (-1, -1, -1, -1, 22, -1, -1, -1)),
    ('hop', (-1, -1, -1, -1, 26, -1, -1, -1)),
    ('hop', (-1, -1, -1, -1, 30, -1, -1, -1)),
    ('wait', (-1, -1, -1, -1, -1, -1, 0, 0)),
    ('grad', (-1, 2, -1, -1, -1, -1, 0, 0)),
    ('own', 'd0', (3,)),
    ('own', 'u1', (3,)),
    ('hop', (-1, -1, -1, -1, -1, 18, -1, -1)),
    ('hop', (-1, -1, -1, -1, -1, 22, -1, -1)),
    ('hop', (-1, -1, -1, -1, -1, 26, -1, -1)),
    ('hop', (-1, -1, -1, -1, -1, 30, -1, -1)),
    ('wait', (-1, 1, -1, -1, -1, -1, -1, -1)),
    ('adj', (0, 1, -1, -1, -1, -1, 0, 0)),
    ('grad', (-1, 1, -1, -1, -1, -1, -1, -1)),
    ('pre', (1, 0, 1, 1, 1, 1, 1, 1)),
    ('fin', (1, 0, 1, 1, 1, 1, 1, 1), (0, 1, 3, 6, 7)),
)
CROSSING = (((0, 0, 0, 0), (1, 1, 0, 0)), ((3, 3, 3, 3), (3, 3, 2, 3)))


def discount_of(section):
    return jnp.exp(section.astype(jnp.float32) * jnp.log(jnp.float32(discount_rate)))


def gathered(expected_cot, value_next, transition, section):
    discount_factor = discount_of(section[0])
    cotangent_all = lax.all_gather(expected_cot, "markov", axis=0, tiled=True)
    adjoint_sum = lax.dot_general(
        lax.all_gather(transition, ("storage", "sub"), axis=0, tiled=True),
        cotangent_all,
        (((0,), (0,)), ((), ())),
        preferred_element_type=jnp.float32,
    )
    own_states = lax.all_to_all(
        cotangent_all, ("storage", "sub"), split_axis=0, concat_axis=1, tiled=True
    )
    gathered_values = lax.all_gather(value_next, ("storage", "sub"), axis=1, tiled=True)
    gradient_sum = lax.dot_general(
        own_states, gathered_values, (((1,), (1,)), ((), ())), preferred_element_type=jnp.float32
    )
    return (discount_factor * adjoint_sum, discount_factor * gradient_sum)


def pick(place, table):
    if len(set(table)) == 1:
        return table[0]
    value = table[0]
    for i, entry in enumerate(table[1:], 1):
        if entry != table[0]:
            value = jnp.where(place == i, entry, value)
    return value


def where(place, places, body):
    if len(places) == 8:
        body()
        return
    among = place == places[0]
    for i in places[1:]:
        among = among | (place == i)
    pl.when(among)(body)


def filled(table):
    return tuple(i for i, entry in enumerate(table) if entry >= 0)


def coded(value, out):
    top = jnp.maximum(jnp.max(jnp.abs(value), axis=0, keepdims=True), 2.0**-100)
    power = jnp.clip(jnp.ceil(jnp.log2(top * 1.0001)), -100, 100)
    whole = jnp.round(value * jnp.exp2(BITS - 1.0 - power)).astype(jnp.int32)
    low = whole & (BASE - 1)
    out[:TILE, :] = ((whole - low) >> (BITS - 16)).astype(jnp.int16)
    n = TILE // SHARE
    packed = low[:n] - 32768
    for i in range(1, SHARE):
        packed = packed + BASE**i * low[i * n : (i + 1) * n]
    out[TILE : TILE + n, :] = packed.astype(jnp.int16)
    out[TILE + n :, :] = jnp.broadcast_to(power.astype(jnp.int32), (16, value.shape[1])).astype(jnp.int16)


def decoded(message):
    n = TILE // SHARE
    high = message[:TILE, :].astype(jnp.int32) * BASE
    low = message[TILE : TILE + n, :].astype(jnp.int32) + 32768
    power = message[TILE + n :, :].astype(jnp.int32)[:1].astype(jnp.float32)
    unit = jnp.exp2(power - (BITS - 1.0))
    return [
        (high[i * n : (i + 1) * n] + ((low >> (BITS - 16) * i) & (BASE - 1))).astype(jnp.float32) * unit
        for i in range(SHARE)
    ]


def kernel(
    section, c_in, v_in, t_in, adj, grad, c_all, c_pair, t_own, t_pair, v_all, p_out, p_in,
    c_recv, up_send, down_send, own_send, own_extra, pair_send, pair_recv,
    v_send, v_recv, t_sems, p_send, p_recv,
):
    g, m = lax.axis_index("groups"), lax.axis_index("markov")
    s, u = lax.axis_index("storage"), lax.axis_index("sub")
    far = 1 - s
    j, p, o, q = 2 * s + u, 2 * s + 1 - u, 2 * far + u, 2 * far + 1 - u
    step = 1 - 2 * s
    z = m + s * (3 - 2 * m)
    row = u + s * (1 - 2 * u)
    place = 2 * z + row
    partner, across = (g, m, s, 1 - u), (g, m, far, u)
    home = lax.rem(m, 2)

    def column(to, side, core):
        return (g, jnp.clip(to, 0, 3), side, core)

    above, below = column(m + step, s, u), column(m - step, s, u)
    up_home, down_home = column(m + step, s, home), column(m - step, s, home)
    states, half = c_all.shape[1:]
    tall = states // PIECES
    following = grad.shape[1]
    is_a, is_b = (z <= 1) & (row == z), (z <= 1) & (row != z)
    pairs = [(h, r) for h in range(2) for r in range(PIECES)]

    def remote(src, dst, send, recv, to):
        return pltpu.make_async_remote_copy(
            src_ref=src, dst_ref=dst, send_sem=send, recv_sem=recv, device_id=to, device_id_type=MESH
        )

    def quarter(c):
        if isinstance(c, int):
            return (j, p, o, q)[c]
        return jnp.where(c == 0, j, jnp.where(c == 1, p, jnp.where(c == 2, o, q)))

    def chunk(code):
        return 2 * quarter(code // 2) + code % 2

    def held(k, r):
        return c_all.at[k, pl.ds(pl.multiple_of(r * tall, tall), tall)]

    def mine(h, r):
        return c_in.at[pl.ds(r * tall, tall), pl.ds(h * half, half)]

    def got(k, r):
        remote(held(k, r), held(k, r), c_recv.at[k, r], c_recv.at[k, r], partner).wait_recv()

    def z_copy(k, r, send, to):
        return remote(held(k, r), held(k, r), send.at[k, r], c_recv.at[k, r], to)

    def own_copy(h, r, send, to):
        return remote(mine(h, r), held(2 * j + h, r), send, c_recv.at[2 * j + h, r], to)

    def own_up(h, r):
        return own_copy(h, r, own_send.at[h, r], up_home)

    def own_down(h, r):
        return own_copy(h, r, own_extra.at[h, r], down_home)

    def own_far(h, r):
        at = jnp.where(z == 3, CROSSING[0][h][r], CROSSING[1][h][r])
        return own_copy(h, r, own_send.at[h, r], column(m + step * (3 - z - at), far, home))

    def own_ahead(h, r):
        return own_copy(h, r, own_extra.at[2 + h, r], column(m + 2 * step, s, home))

    def own_pair(h, r):
        return own_copy(h, r, own_extra.at[2 + h, r], partner)

    def pair_copy(i):
        k = (2 * q, 2 * q + 1, 2 * p, 2 * p + 1)[i]
        return remote(c_all.at[k], c_pair.at[i], pair_send.at[i], pair_recv.at[i], partner)

    def pair_got(i):
        remote(c_pair.at[i], c_pair.at[i], pair_recv.at[i], pair_recv.at[i], partner).wait_recv()

    def v_half(h):
        return v_in.at[:, pl.ds(h * half, half)]

    def v_across(h):
        return remote(v_half(h), v_all.at[2 * j + h], v_send.at[h], v_recv.at[h], across)

    def v_relay():
        part = v_all.at[pl.ds(2 * o, 2)]
        return remote(part, part, v_send.at[2], v_recv.at[2], partner)

    def v_pair(h):
        return remote(v_half(h), v_all.at[2 * j + h], v_send.at[3 + h], v_recv.at[3 + h], partner)

    def t_copy():
        return remote(t_in, t_pair, t_sems.at[0], t_sems.at[1], partner)

    def p_copy(h, n):
        return remote(p_out.at[h, n], p_in.at[h, n], p_send.at[h, n], p_recv.at[h, n], across)

    barrier = pltpu.get_barrier_semaphore()
    for dz in range(4):
        for dc in range(4):
            if dz or dc:
                to = (g, lax.rem(m + dz, 4), lax.rem(s + dc // 2, 2), lax.rem(u + dc % 2, 2))
                pl.semaphore_signal(barrier, inc=1, device_id=to, device_id_type=MESH)

    locals_ = [pltpu.make_async_copy(t_in, t_own, t_sems.at[2])]
    for h in range(2):
        locals_.append(pltpu.make_async_copy(v_half(h), v_all.at[2 * j + h], t_sems.at[3 + h]))

    @pl.when(is_a)
    def _():
        for h, r in pairs:
            pltpu.make_async_copy(mine(h, r), held(2 * j + h, r), c_recv.at[2 * j + h, r]).start()

    for copy in locals_:
        copy.start()
    pl.semaphore_wait(barrier, 15)

    def hop(table):
        def body():
            code = pick(place, tuple(entry // 4 for entry in table))
            k, r = chunk(code // PIECES), code % PIECES
            got(k, r)
            ups = tuple(i for i in filled(table) if table[i] % 4 >= 2)
            downs = tuple(i for i in filled(table) if table[i] % 2)
            if ups:
                where(place, ups, lambda: z_copy(k, r, up_send, above).start())
            if downs:
                where(place, downs, lambda: z_copy(k, r, down_send, below).start())

        where(place, filled(table), body)

    def bulk(table):
        def body():
            k = chunk(pick(place, table))
            for r in range(PIECES):
                got(k, r)

        where(place, filled(table), body)

    def own(name, places):
        copy, h = {"u": own_up, "d": own_down, "f": own_far, "x": own_ahead}[name[0]], int(name[1])

        def body():
            for r in range(AHEAD if name[0] == "x" else PIECES):
                copy(h, r).start()

        where(place, places, body)

    def both(t_block, at, c_block):
        return lax.dot_general(
            t_block[:, at], c_block[...], (((0,), (0,)), ((), ())), preferred_element_type=jnp.float32
        )

    def part(table):
        def body():
            h = pick(place, table)
            pair_got(h)

            @pl.loop(0, following // TILE)
            def _(n):
                at = pl.ds(pl.multiple_of(n * TILE, TILE), TILE)
                value = both(t_own, at, c_all.at[2 * o + h]) + both(t_pair, at, c_pair.at[h])
                coded(value, p_out.at[h, n])
                p_copy(h, n).start()

        where(place, filled(table), body)

    def adjoint(table, factor):
        def body():
            h = pick(place, table)
            pair_got(2 + h)
            cut = pl.ds(pl.multiple_of(h * half, half), half)

            @pl.loop(0, following // TILE)
            def _(n):
                at = pl.ds(pl.multiple_of(n * TILE, TILE), TILE)
                value = both(t_own, at, c_all.at[2 * j + h]) + both(t_pair, at, c_pair.at[2 + h])
                p_copy(h, n).wait_recv()
                tall = TILE // SHARE
                for i, part in enumerate(decoded(p_in.at[h, n])):
                    rows = pl.ds(pl.multiple_of(n * TILE + i * tall, tall), tall)
                    adj[rows, cut] = factor * (value[i * tall : (i + 1) * tall] + part)

        where(place, filled(table), body)

    def product(k, at):
        return lax.dot_general(
            c_all[k, at, :], v_all[k], (((1,), (1,)), ((), ())), preferred_element_type=jnp.float32
        )

    def gradient(table, first):
        def body():
            k = chunk(pick(place, table))

            @pl.loop(0, states // TALL)
            def _(n):
                at = pl.ds(pl.multiple_of(n * TALL, TALL), TALL)
                grad[at, :] = product(k, at) if first else grad[at, :] + product(k, at)

        where(place, filled(table), body)

    tiles = following // TILE

    def cut_of(h):
        return pl.ds(pl.multiple_of(h * half, half), half)

    def add_partial(h, n, scale):
        p_copy(h, n).wait_recv()
        top = TILE // SHARE
        for i, value in enumerate(decoded(p_in.at[h, n])):
            at = pl.ds(n * TILE + i * top, top)
            adj[at, cut_of(h)] = scale(adj[at, cut_of(h)] + value)

    def begin(table):
        h = pick(place, table)
        pair_got(2 + h)

        @pl.loop(0, tiles)
        def _(n):
            at = pl.ds(pl.multiple_of(n * TILE, TILE), TILE)
            adj[at, cut_of(h)] = both(t_pair, at, c_pair.at[2 + h])

        for n in range(tiles - 1):
            add_partial(h, n, lambda value: value)

    def finish(table, late, factor):
        h = pick(place, table)
        k = 2 * j + h

        @pl.loop(0, PIECES)
        def _(r):
            where(place, late, lambda: got(k, r))
            at = pl.ds(pl.multiple_of(r * tall, tall), tall)
            grad[at, :] = factor * (grad[at, :] + product(k, at))
            adj[:, cut_of(h)] += lax.dot_general(
                t_own[at, :], c_all[k, at, :], (((0,), (0,)), ((), ())),
                preferred_element_type=jnp.float32,
            )

        done = pl.ds(0, (tiles - 1) * TILE)
        adj[done, cut_of(h)] = factor * adj[done, cut_of(h)]
        add_partial(h, tiles - 1, lambda value: factor * value)

    @pl.when(is_b)
    def _():
        for h, r in pairs:
            own_pair(h, r).start()

    t_copy().start()
    for h in range(2):
        v_pair(h).start()
    ready, graded = False, False
    for kind, *rest in PLAN:
        if kind in ("part", "grad") and not ready:
            ready = True
            factor = jnp.max(discount_of(jnp.full((8, 128), section[0])))
            for copy in locals_:
                copy.wait()
            t_copy().wait_recv()
            for h in range(2):
                v_pair(h).wait_recv()
        if kind == "hop":
            hop(*rest)
        elif kind == "wait":
            bulk(*rest)
        elif kind == "own":
            own(*rest)
        elif kind == "v":
            where(place, rest[1], lambda: v_across(rest[0]).start())
        elif kind == "pair":
            where(place, rest[1], lambda: pair_copy(rest[0]).start())
        elif kind == "part":
            part(*rest)
        elif kind == "relay":
            for h in range(2):
                v_across(h).wait_recv()
            v_relay().start()
        elif kind == "v_q":
            where(place, rest[0], lambda: v_relay().wait_recv())
        elif kind == "grad":
            gradient(*rest, not graded)
            graded = True
        elif kind == "adj":
            adjoint(*rest, factor)
        elif kind == "pre":
            begin(*rest)
        else:
            finish(*rest, factor)

    for h, r in pairs:
        own_up(h, r).wait_send()

        @pl.when((z == 1))
        def _():
            own_down(h, r).wait_send()

        @pl.when(is_b)
        def _():
            own_pair(h, r).wait_send()

    for r in range(AHEAD):
        pl.when(is_a & (z == 1))(lambda: own_ahead(0, r).wait_send())

    ups, downs = {}, {}
    for kind, *rest in PLAN:
        if kind == "hop":
            for i, entry in enumerate(rest[0]):
                if entry >= 0 and entry % 4 >= 2:
                    ups.setdefault(entry // 4, []).append(i)
                if entry >= 0 and entry % 2:
                    downs.setdefault(entry // 4, []).append(i)
    for sent, send in ((ups, up_send), (downs, down_send)):
        for code in sorted(sent):
            k, r = chunk(code // PIECES), code % PIECES
            where(place, sent[code], lambda: z_copy(k, r, send, above).wait_send())
    for i in range(4):
        pair_copy(i).wait_send()
    for h in range(2):
        v_across(h).wait_send()
        v_pair(h).wait_send()
    v_relay().wait_send()
    t_copy().wait_send()
    for h in range(2):
        for n in range(following // TILE):
            p_copy(h, n).wait_send()


def stored(adj, grad, adj_out, grad_out, sems):
    copies = []
    for i, (src, dst) in enumerate(((grad, grad_out), (adj, adj_out))):
        tall = src.shape[0] // STREAMS
        for n in range(STREAMS):
            at = pl.ds(n * tall, tall)
            copies.append(pltpu.make_async_copy(src.at[at], dst.at[at], sems.at[i, n]))
    for copy in copies:
        copy.start()
    for copy in copies:
        copy.wait()


def exchanged(expected_cot, value_next, transition, section):
    states, cells = expected_cot.shape
    current, following = transition.shape
    dma = pltpu.SemaphoreType.DMA
    half = cells // 2
    tiles = following // TILE
    arrays = (expected_cot, value_next, transition)
    sums = pl.pallas_call(
        kernel,
        out_shape=(
            jax.ShapeDtypeStruct((following, cells), jnp.float32),
            jax.ShapeDtypeStruct((current, following), jnp.float32),
        ),
        in_specs=[pl.BlockSpec(memory_space=pltpu.SMEM)] + [pl.BlockSpec(memory_space=pltpu.HBM)] * 3,
        out_specs=(pl.BlockSpec(memory_space=pltpu.VMEM),) * 2,
        scratch_shapes=[
            pltpu.VMEM((8, states, half), jnp.bfloat16),
            pltpu.VMEM((4, states, half), jnp.bfloat16),
            pltpu.VMEM((current, following), jnp.bfloat16),
            pltpu.VMEM((current, following), jnp.bfloat16),
            pltpu.VMEM((8, states, half), jnp.bfloat16),
            pltpu.VMEM((2, tiles, MESSAGE, half), jnp.int16),
            pltpu.VMEM((2, tiles, MESSAGE, half), jnp.int16),
            dma((8, PIECES)),
            dma((8, PIECES)),
            dma((8, PIECES)),
            dma((2, PIECES)),
            dma((4, PIECES)),
            dma((4,)),
            dma((4,)),
            dma((5,)),
            dma((5,)),
            dma((5,)),
            dma((2, tiles)),
            dma((2, tiles)),
        ],
        compiler_params=pltpu.CompilerParams(
            collective_id=0, has_side_effects=True, vmem_limit_bytes=VMEM_BYTES
        ),
    )(section, *(pltpu.with_memory_space_constraint(x, pltpu.HBM) for x in arrays))
    return pl.pallas_call(
        stored,
        out_shape=tuple(jax.ShapeDtypeStruct(x.shape, x.dtype) for x in sums),
        in_specs=[pl.BlockSpec(memory_space=pltpu.VMEM)] * 2,
        out_specs=(pl.BlockSpec(memory_space=pltpu.HBM),) * 2,
        scratch_shapes=[dma((2, STREAMS))],
        compiler_params=pltpu.CompilerParams(vmem_limit_bytes=1024 * 1024),
    )(*(pltpu.with_memory_space_constraint(x, pltpu.VMEM) for x in sums))


def solution(mesh):
    shape = mesh.shape
    paired = shape["storage"] == 2 and shape["sub"] == 2 and shape["markov"] == 4
    body = exchanged if paired else gathered
    return jax.shard_map(
        body,
        mesh=mesh,
        in_specs=(
            P(("groups", "markov"), ("storage", "sub")),
            P(("groups", "markov"), ("storage", "sub")),
            P(("groups", "storage", "sub"), "markov"),
            P("groups"),
        ),
        out_specs=(
            P(("groups", "markov"), ("storage", "sub")),
            P(("groups", "storage", "sub"), "markov"),
        ),
        check_vma=False,
    )
```

```python
import jax
import jax.numpy as jnp
from jax import lax
from jax.experimental import pallas as pl
from jax.experimental.pallas import tpu as pltpu
from jax.sharding import PartitionSpec as P

discount_rate = 0.97
MESH = pl.DeviceIdType.MESH
PIECES = 4
TILE = 256
TALL = 512
STORE_BYTES = 6 * 1024 * 1024
AHEAD = 0
BITS = 20
BASE = 2 ** (BITS - 16)
SHARE = 16 // (BITS - 16)
MESSAGE = TILE + TILE // SHARE + 16
VMEM_BYTES = 30 * 1024 * 1024

PLAN = (
    ('wait', (2, -1, -1, -1, -1, -1, -1, -1)),
    ('pair', 2, (0,)),
    ('v', 1, (1, 3)),
    ('own', 'u0', (2,)),
    ('v', 0, (4, 5)),
    ('own', 'f1', (6, 7)),
    ('wait', (3, -1, -1, -1, -1, -1, -1, -1)),
    ('pair', 3, (0,)),
    ('v', 0, (1,)),
    ('own', 'u1', (2,)),
    ('wait', (-1, -1, -1, 2, -1, -1, -1, -1)),
    ('pair', 2, (3,)),
    ('v', 1, (4, 5)),
    ('own', 'f0', (6, 7)),
    ('own', 'u0', (1,)),
    ('v', 1, (2, 6, 7)),
    ('wait', (-1, -1, -1, 3, -1, -1, -1, -1)),
    ('pair', 3, (3,)),
    ('own', 'f0', (4, 5)),
    ('own', 'u1', (1,)),
    ('v', 0, (3, 6)),
    ('own', 'f1', (4,)),
    ('wait', (-1, -1, -1, -1, -1, -1, 7, -1)),
    ('pair', 1, (6,)),
    ('hop', (82, -1, 87, 97, 86, 34, -1, 97)),
    ('hop', (114, -1, 119, 65, 118, 38, -1, 65)),
    ('hop', (90, -1, 82, 101, 82, 42, -1, 101)),
    ('wait', (-1, -1, -1, -1, -1, -1, -1, 2)),
    ('pair', 2, (7,)),
    ('hop', (122, -1, 95, 69, 94, 46, -1, 69)),
    ('pair', 2, (5,)),
    ('hop', (66, -1, 114, 105, 114, 50, -1, 105)),
    ('own', 'f1', (5,)),
    ('hop', (98, -1, 127, -1, 126, 54, -1, 73)),
    ('hop', (70, -1, 90, -1, 90, 97, -1, 109)),
    ('v', 1, (0,)),
    ('pair', 0, (7,)),
    ('wait', (-1, -1, -1, -1, -1, -1, -1, 3)),
    ('pair', 3, (7,)),
    ('hop', (102, -1, 122, -1, 122, 58, -1, 77)),
    ('pair', 1, (2, 4)),
    ('hop', (74, -1, 66, -1, 66, 65, -1, 113)),
    ('v', 0, (0,)),
    ('hop', (106, -1, 98, -1, 98, 62, -1, 81)),
    ('v', 0, (2,)),
    ('pair', 3, (5,)),
    ('hop', (78, -1, 70, -1, 70, 101, -1, 117)),
    ('hop', (110, -1, 102, -1, 102, 69, -1, 85)),
    ('pair', 0, (0,)),
    ('hop', (84, -1, 74, -1, 74, 105, -1, 121)),
    ('hop', (116, -1, 106, -1, 106, 73, -1, 89)),
    ('v', 0, (7,)),
    ('hop', (92, -1, 78, -1, -1, 109, -1, 124)),
    ('own', 'u0', (0,)),
    ('pair', 0, (5,)),
    ('pair', 1, (7,)),
    ('own', 'u1', (0,)),
    ('hop', (124, -1, 110, -1, -1, 77, -1, 92)),
    ('pair', 1, (0,)),
    ('pair', 0, (2,)),
    ('hop', (-1, -1, 34, -1, -1, 113, -1, -1)),
    ('hop', (-1, -1, 38, -1, -1, 81, -1, -1)),
    ('hop', (-1, -1, 42, -1, -1, 117, -1, -1)),
    ('hop', (-1, -1, 46, -1, -1, 85, -1, -1)),
    ('pair', 2, (2,)),
    ('hop', (-1, -1, 50, -1, -1, 127, -1, -1)),
    ('hop', (-1, -1, 54, -1, -1, 121, -1, -1)),
    ('hop', (-1, -1, -1, -1, -1, 95, -1, -1)),
    ('pair', 1, (5,)),
    ('hop', (-1, -1, -1, -1, -1, 89, -1, -1)),
    ('wait', (-1, -1, -1, -1, -1, -1, 5, -1)),
    ('part', (-1, -1, -1, -1, 1, 1, 1, 1)),
    ('hop', (-1, -1, 2, 73, 78, -1, -1, -1)),
    ('hop', (-1, -1, 58, 109, 110, -1, -1, -1)),
    ('pair', 0, (3, 4)),
    ('hop', (-1, -1, 6, -1, -1, -1, -1, -1)),
    ('relay',),
    ('wait', (-1, 6, -1, -1, -1, -1, -1, -1)),
    ('pair', 0, (1,)),
    ('hop', (-1, -1, 62, 77, 34, -1, -1, -1)),
    ('pair', 3, (2,)),
    ('hop', (-1, -1, 10, 113, 38, -1, -1, -1)),
    ('own', 'd1', (2,)),
    ('own', 'u0', (3,)),
    ('hop', (-1, -1, 14, -1, 42, -1, -1, -1)),
    ('wait', (-1, -1, -1, -1, -1, -1, 4, -1)),
    ('part', (-1, -1, 0, 0, 0, 0, 0, -1)),
    ('wait', (-1, -1, -1, -1, -1, -1, 6, -1)),
    ('pair', 0, (6,)),
    ('hop', (-1, -1, 18, 81, 46, -1, -1, -1)),
    ('pair', 2, (4,)),
    ('hop', (-1, -1, 22, 117, -1, -1, -1, -1)),
    ('hop', (-1, -1, -1, 85, -1, -1, -1, -1)),
    ('wait', (-1, 4, -1, -1, -1, -1, -1, -1)),
    ('part', (0, 0, -1, -1, -1, -1, -1, -1)),
    ('hop', (-1, -1, 26, 125, 50, 2, -1, -1)),
    ('wait', (1, -1, -1, 1, -1, -1, -1, -1)),
    ('v_q', (1,)),
    ('grad', (1, 6, 5, 1, 5, 2, 5, 2)),
    ('v_q', (2, 4, 6)),
    ('grad', (2, 4, 7, 2, 7, 3, 7, 3)),
    ('hop', (-1, -1, 30, 121, 54, 6, -1, -1)),
    ('pair', 1, (3,)),
    ('hop', (-1, -1, -1, 93, -1, -1, -1, -1)),
    ('part', (-1, -1, -1, -1, -1, -1, -1, 0)),
    ('wait', (-1, 3, -1, -1, -1, -1, -1, -1)),
    ('pair', 3, (1,)),
    ('wait', (-1, -1, -1, -1, -1, -1, 2, -1)),
    ('pair', 2, (6,)),
    ('hop', (-1, -1, -1, 89, 2, 10, -1, -1)),
    ('hop', (-1, -1, -1, -1, 58, 14, -1, -1)),
    ('hop', (-1, -1, -1, -1, 6, -1, -1, -1)),
    ('v_q', (5, 7)),
    ('grad', (3, 3, 4, 3, 4, 6, 4, 6)),
    ('wait', (-1, 7, -1, -1, -1, -1, -1, -1)),
    ('pair', 1, (1,)),
    ('hop', (-1, -1, -1, -1, 62, -1, -1, -1)),
    ('pair', 3, (4,)),
    ('v_q', (3,)),
    ('grad', (4, 7, 6, 6, 6, 4, 6, 4)),
    ('v_q', (0,)),
    ('grad', (6, -1, 2, 4, 2, 7, 2, 7)),
    ('hop', (-1, -1, -1, -1, 10, -1, -1, -1)),
    ('hop', (-1, -1, -1, -1, 14, -1, -1, -1)),
    ('wait', (-1, 5, -1, -1, -1, -1, -1, -1)),
    ('grad', (5, 5, 3, 7, 3, 5, -1, 5)),
    ('wait', (-1, -1, -1, -1, -1, -1, -1, 0)),
    ('grad', (7, -1, 1, 5, 0, 0, -1, 0)),
    ('hop', (-1, -1, -1, -1, 18, -1, -1, -1)),
    ('part', (1, 1, 1, 1, -1, -1, -1, -1)),
    ('adj', (1, -1, 1, 1, 0, 0, -1, -1)),
    ('wait', (-1, 2, -1, -1, -1, -1, -1, -1)),
    ('pair', 2, (1,)),
    ('own', 'd0', (2,)),
    ('wait', (-1, -1, -1, -1, -1, -1, 3, -1)),
    ('pair', 3, (6,)),
    ('hop', (-1, -1, -1, -1, 22, -1, -1, -1)),
    ('hop', (-1, -1, -1, -1, 26, -1, -1, -1)),
    ('hop', (-1, -1, -1, -1, 30, -1, -1, -1)),
    ('grad', (-1, 2, -1, -1, -1, -1, 3, -1)),
    ('own', 'd1', (3,)),
    ('own', 'd0', (3,)),
    ('own', 'u1', (3,)),
    ('hop', (-1, -1, -1, -1, -1, 18, -1, -1)),
    ('hop', (-1, -1, -1, -1, -1, 22, -1, -1)),
    ('hop', (-1, -1, -1, -1, -1, 26, -1, -1)),
    ('hop', (-1, -1, -1, -1, -1, 30, -1, -1)),
    ('wait', (-1, 1, -1, -1, -1, -1, 0, -1)),
    ('adj', (-1, 1, -1, -1, -1, -1, 0, 0)),
    ('grad', (-1, 1, -1, -1, -1, -1, 0, -1)),
    ('pre', (0, 0, 0, 0, 1, 1, 1, 1)),
    ('fin', (0, 0, 0, 0, 1, 1, 1, 1), (0, 1, 3, 6, 7)),
)
CROSSING = (((0, 0, 0, 0), (0, 1, 0, 1)), ((3, 3, 3, 3), (3, 3, 3, 2)))


def discount_of(section):
    return jnp.exp(section.astype(jnp.float32) * jnp.log(jnp.float32(discount_rate)))


def gathered(expected_cot, value_next, transition, section):
    discount_factor = discount_of(section[0])
    cotangent_all = lax.all_gather(expected_cot, "markov", axis=0, tiled=True)
    adjoint_sum = lax.dot_general(
        lax.all_gather(transition, ("storage", "sub"), axis=0, tiled=True),
        cotangent_all,
        (((0,), (0,)), ((), ())),
        preferred_element_type=jnp.float32,
    )
    own_states = lax.all_to_all(
        cotangent_all, ("storage", "sub"), split_axis=0, concat_axis=1, tiled=True
    )
    gathered_values = lax.all_gather(value_next, ("storage", "sub"), axis=1, tiled=True)
    gradient_sum = lax.dot_general(
        own_states, gathered_values, (((1,), (1,)), ((), ())), preferred_element_type=jnp.float32
    )
    return (discount_factor * adjoint_sum, discount_factor * gradient_sum)


def pick(place, table):
    if len(set(table)) == 1:
        return table[0]
    value = table[0]
    for i, entry in enumerate(table[1:], 1):
        if entry != table[0]:
            value = jnp.where(place == i, entry, value)
    return value


def where(place, places, body):
    if len(places) == 8:
        body()
        return
    among = place == places[0]
    for i in places[1:]:
        among = among | (place == i)
    pl.when(among)(body)


def filled(table):
    return tuple(i for i, entry in enumerate(table) if entry >= 0)


def coded(value, out):
    top = jnp.maximum(jnp.max(jnp.abs(value), axis=0, keepdims=True), 2.0**-100)
    power = jnp.clip(jnp.ceil(jnp.log2(top * 1.0001)), -100, 100)
    whole = jnp.round(value * jnp.exp2(BITS - 1.0 - power)).astype(jnp.int32)
    low = whole & (BASE - 1)
    out[:TILE, :] = ((whole - low) >> (BITS - 16)).astype(jnp.int16)
    n = TILE // SHARE
    packed = low[:n] - 32768
    for i in range(1, SHARE):
        packed = packed + BASE**i * low[i * n : (i + 1) * n]
    out[TILE : TILE + n, :] = packed.astype(jnp.int16)
    out[TILE + n :, :] = jnp.broadcast_to(power.astype(jnp.int32), (16, value.shape[1])).astype(jnp.int16)


def decoded(message):
    n = TILE // SHARE
    high = message[:TILE, :].astype(jnp.int32) * BASE
    low = message[TILE : TILE + n, :].astype(jnp.int32) + 32768
    power = message[TILE + n :, :].astype(jnp.int32)[:1].astype(jnp.float32)
    unit = jnp.exp2(power - (BITS - 1.0))
    return [
        (high[i * n : (i + 1) * n] + ((low >> (BITS - 16) * i) & (BASE - 1))).astype(jnp.float32) * unit
        for i in range(SHARE)
    ]


def kernel(
    section, c_in, v_in, t_in, adj, grad, c_all, v_all, t_own, p_in, c_pair, t_pair, p_out,
    c_recv, up_send, down_send, own_send, own_extra, pair_send, pair_recv,
    v_send, v_recv, t_sems, p_send, p_recv,
):
    g, m = lax.axis_index("groups"), lax.axis_index("markov")
    s, u = lax.axis_index("storage"), lax.axis_index("sub")
    far = 1 - s
    j, p, o, q = 2 * s + u, 2 * s + 1 - u, 2 * far + u, 2 * far + 1 - u
    step = 1 - 2 * s
    z = m + s * (3 - 2 * m)
    row = u + s * (1 - 2 * u)
    place = 2 * z + row
    partner, across = (g, m, s, 1 - u), (g, m, far, u)
    home = lax.rem(m, 2)

    def column(to, side, core):
        return (g, jnp.clip(to, 0, 3), side, core)

    above, below = column(m + step, s, u), column(m - step, s, u)
    up_home, down_home = column(m + step, s, home), column(m - step, s, home)
    states, half = c_all.shape[1:]
    tall = states // PIECES
    following = grad.shape[1]
    is_a, is_b = (z <= 1) & (row == z), (z <= 1) & (row != z)
    pairs = [(h, r) for h in range(2) for r in range(PIECES)]

    def remote(src, dst, send, recv, to):
        return pltpu.make_async_remote_copy(
            src_ref=src, dst_ref=dst, send_sem=send, recv_sem=recv, device_id=to, device_id_type=MESH
        )

    def quarter(c):
        if isinstance(c, int):
            return (j, p, o, q)[c]
        return jnp.where(c == 0, j, jnp.where(c == 1, p, jnp.where(c == 2, o, q)))

    def chunk(code):
        return 2 * quarter(code // 2) + code % 2

    def held(k, r):
        return c_all.at[k, pl.ds(pl.multiple_of(r * tall, tall), tall)]

    def mine(h, r):
        return c_in.at[pl.ds(r * tall, tall), pl.ds(h * half, half)]

    def got(k, r):
        remote(held(k, r), held(k, r), c_recv.at[k, r], c_recv.at[k, r], partner).wait_recv()

    def z_copy(k, r, send, to):
        return remote(held(k, r), held(k, r), send.at[k, r], c_recv.at[k, r], to)

    def own_copy(h, r, send, to):
        return remote(mine(h, r), held(2 * j + h, r), send, c_recv.at[2 * j + h, r], to)

    def own_up(h, r):
        return own_copy(h, r, own_send.at[h, r], up_home)

    def own_down(h, r):
        return own_copy(h, r, own_extra.at[h, r], down_home)

    def own_far(h, r):
        at = jnp.where(z == 3, CROSSING[0][h][r], CROSSING[1][h][r])
        return own_copy(h, r, own_send.at[h, r], column(m + step * (3 - z - at), far, home))

    def own_ahead(h, r):
        return own_copy(h, r, own_extra.at[2 + h, r], column(m + 2 * step, s, home))

    def own_pair(h, r):
        return own_copy(h, r, own_extra.at[2 + h, r], partner)

    def pair_copy(i):
        k = (2 * q, 2 * q + 1, 2 * p, 2 * p + 1)[i]
        return remote(c_all.at[k], c_pair.at[i], pair_send.at[i], pair_recv.at[i], partner)

    def pair_got(i):
        remote(c_pair.at[i], c_pair.at[i], pair_recv.at[i], pair_recv.at[i], partner).wait_recv()

    def v_half(h):
        return v_in.at[:, pl.ds(h * half, half)]

    def v_across(h):
        return remote(v_half(h), v_all.at[2 * j + h], v_send.at[h], v_recv.at[h], across)

    def v_relay():
        part = v_all.at[pl.ds(2 * o, 2)]
        return remote(part, part, v_send.at[2], v_recv.at[2], partner)

    def v_pair(h):
        return remote(v_half(h), v_all.at[2 * j + h], v_send.at[3 + h], v_recv.at[3 + h], partner)

    def t_copy():
        return remote(t_in, t_pair, t_sems.at[0], t_sems.at[1], partner)

    def p_copy(h, n):
        return remote(p_out.at[h, n], p_in.at[h, n], p_send.at[h, n], p_recv.at[h, n], across)

    barrier = pltpu.get_barrier_semaphore()
    for dz in range(4):
        for dc in range(4):
            if dz or dc:
                to = (g, lax.rem(m + dz, 4), lax.rem(s + dc // 2, 2), lax.rem(u + dc % 2, 2))
                pl.semaphore_signal(barrier, inc=1, device_id=to, device_id_type=MESH)

    locals_ = [pltpu.make_async_copy(t_in, t_own, t_sems.at[2])]
    for h in range(2):
        locals_.append(pltpu.make_async_copy(v_half(h), v_all.at[2 * j + h], t_sems.at[3 + h]))

    @pl.when(is_a)
    def _():
        for h, r in pairs:
            pltpu.make_async_copy(mine(h, r), held(2 * j + h, r), c_recv.at[2 * j + h, r]).start()

    for copy in locals_:
        copy.start()
    pl.semaphore_wait(barrier, 15)

    def hop(table):
        def body():
            code = pick(place, tuple(entry // 4 for entry in table))
            k, r = chunk(code // PIECES), code % PIECES
            got(k, r)
            ups = tuple(i for i in filled(table) if table[i] % 4 >= 2)
            downs = tuple(i for i in filled(table) if table[i] % 2)
            if ups:
                where(place, ups, lambda: z_copy(k, r, up_send, above).start())
            if downs:
                where(place, downs, lambda: z_copy(k, r, down_send, below).start())

        where(place, filled(table), body)

    def bulk(table):
        def body():
            k = chunk(pick(place, table))
            for r in range(PIECES):
                got(k, r)

        where(place, filled(table), body)

    def own(name, places):
        copy, h = {"u": own_up, "d": own_down, "f": own_far, "x": own_ahead}[name[0]], int(name[1])

        def body():
            for r in range(AHEAD if name[0] == "x" else PIECES):
                copy(h, r).start()

        where(place, places, body)

    def both(t_block, at, c_block):
        return lax.dot_general(
            t_block[:, at], c_block[...], (((0,), (0,)), ((), ())), preferred_element_type=jnp.float32
        )

    def part(table):
        def body():
            h = pick(place, table)
            pair_got(h)

            @pl.loop(0, following // TILE)
            def _(n):
                at = pl.ds(pl.multiple_of(n * TILE, TILE), TILE)
                value = both(t_own, at, c_all.at[2 * o + h]) + both(t_pair, at, c_pair.at[h])
                coded(value, p_out.at[h, n])
                p_copy(h, n).start()

        where(place, filled(table), body)

    def adjoint(table, factor):
        def body():
            h = pick(place, table)
            pair_got(2 + h)
            cut = pl.ds(pl.multiple_of(h * half, half), half)

            @pl.loop(0, following // TILE)
            def _(n):
                at = pl.ds(pl.multiple_of(n * TILE, TILE), TILE)
                value = both(t_own, at, c_all.at[2 * j + h]) + both(t_pair, at, c_pair.at[2 + h])
                p_copy(h, n).wait_recv()
                tall = TILE // SHARE
                for i, part in enumerate(decoded(p_in.at[h, n])):
                    rows = pl.ds(pl.multiple_of(n * TILE + i * tall, tall), tall)
                    adj[rows, cut] = factor * (value[i * tall : (i + 1) * tall] + part)

        where(place, filled(table), body)

    def product(k, at):
        return lax.dot_general(
            c_all[k, at, :], v_all[k], (((1,), (1,)), ((), ())), preferred_element_type=jnp.float32
        )

    def gradient(table, first):
        def body():
            k = chunk(pick(place, table))

            @pl.loop(0, states // TALL)
            def _(n):
                at = pl.ds(pl.multiple_of(n * TALL, TALL), TALL)
                grad[at, :] = product(k, at) if first else grad[at, :] + product(k, at)

        where(place, filled(table), body)

    tiles = following // TILE

    def cut_of(h):
        return pl.ds(pl.multiple_of(h * half, half), half)

    def add_partial(h, n):
        p_copy(h, n).wait_recv()
        top = TILE // SHARE
        for i, value in enumerate(decoded(p_in.at[h, n])):
            at = pl.ds(n * TILE + i * top, top)
            adj[at, cut_of(h)] += value

    def begin(table):
        h = pick(place, table)
        pair_got(2 + h)

        @pl.loop(0, tiles)
        def _(n):
            at = pl.ds(pl.multiple_of(n * TILE, TILE), TILE)
            adj[at, cut_of(h)] = both(t_pair, at, c_pair.at[2 + h])

        for n in range(tiles - 1):
            add_partial(h, n)

    def finish(table, late, factor):
        h = pick(place, table)
        k = 2 * j + h
        late_got = lambda r: where(place, late, lambda: got(k, r)) if late else None

        @pl.loop(0, PIECES - 1)
        def _(r):
            late_got(r)
            at = pl.ds(pl.multiple_of(r * tall, tall), tall)
            grad[at, :] = factor * (grad[at, :] + product(k, at))
            adj[:, cut_of(h)] += lax.dot_general(
                t_own[at, :], c_all[k, at, :], (((0,), (0,)), ((), ())),
                preferred_element_type=jnp.float32,
            )

        late_got(PIECES - 1)
        p_copy(h, tiles - 1).wait_recv()

    def drain_late():
        ups = {}
        for kind, *rest in PLAN:
            if kind == "hop":
                for i, entry in enumerate(rest[0]):
                    if entry >= 0 and entry % 4 >= 2 and entry // 4 < 4 * PIECES:
                        ups.setdefault(entry // 4, []).append(i)
        for code in sorted(ups):
            k, r = chunk(code // PIECES), code % PIECES
            where(place, ups[code], lambda: z_copy(k, r, up_send, above).wait_send())

    def drain():
        for h, r in pairs:
            own_up(h, r).wait_send()

            @pl.when((z == 1))
            def _():
                own_down(h, r).wait_send()

            @pl.when(is_b)
            def _():
                own_pair(h, r).wait_send()

        for r in range(AHEAD):
            pl.when(is_a & (z == 1))(lambda: own_ahead(0, r).wait_send())

        ups, downs = {}, {}
        for kind, *rest in PLAN:
            if kind == "hop":
                for i, entry in enumerate(rest[0]):
                    if entry >= 0 and entry % 4 >= 2 and entry // 4 >= 4 * PIECES:
                        ups.setdefault(entry // 4, []).append(i)
                    if entry >= 0 and entry % 2:
                        downs.setdefault(entry // 4, []).append(i)
        for sent, send in ((ups, up_send), (downs, down_send)):
            for code in sorted(sent):
                k, r = chunk(code // PIECES), code % PIECES
                where(place, sent[code], lambda: z_copy(k, r, send, above).wait_send())
        for i in range(4):
            pair_copy(i).wait_send()
        for h in range(2):
            v_across(h).wait_send()
            v_pair(h).wait_send()
        v_relay().wait_send()
        t_copy().wait_send()

    def begin_pairs():
        @pl.when(is_b)
        def _():
            for h, r in pairs:
                own_pair(h, r).start()

        t_copy().start()
        for h in range(2):
            v_pair(h).start()

    begun, ready, graded = False, False, False
    for kind, *rest in PLAN:
        if kind not in ("own", "v") and not begun:
            begun = True
            begin_pairs()
        if kind in ("part", "grad") and not ready:
            ready = True
            factor = jnp.max(discount_of(jnp.full((8, 128), section[0])))
            for copy in locals_:
                copy.wait()
            t_copy().wait_recv()
            for h in range(2):
                v_pair(h).wait_recv()
        if kind == "hop":
            hop(*rest)
        elif kind == "wait":
            bulk(*rest)
        elif kind == "own":
            own(*rest)
        elif kind == "v":
            where(place, rest[1], lambda: v_across(rest[0]).start())
        elif kind == "pair":
            where(place, rest[1], lambda: pair_copy(rest[0]).start())
        elif kind == "part":
            part(*rest)
        elif kind == "relay":
            for h in range(2):
                v_across(h).wait_recv()
            v_relay().start()
        elif kind == "v_q":
            where(place, rest[0], lambda: v_relay().wait_recv())
        elif kind == "grad":
            gradient(*rest, not graded)
            graded = True
        elif kind == "adj":
            adjoint(*rest, factor)
        elif kind == "pre":
            begin(*rest)
        else:
            drain()
            finish(*rest, factor)
            drain_late()

    for h in range(2):
        for n in range(following // TILE):
            p_copy(h, n).wait_send()


def stored(section, adj, grad, c_all, v_all, t_own, p_in, adj_out, grad_out, grad_last, adj_last, sems):
    m, s, u = (lax.axis_index(name) for name in ("markov", "storage", "sub"))
    place = 2 * (m + s * (3 - 2 * m)) + u + s * (1 - 2 * u)
    h = pick(place, PLAN[-1][1])
    k = 2 * (2 * s + u) + h
    states, half = c_all.shape[1:]
    kept = states - states // PIECES
    last = pl.ds(kept, states - kept)
    cut = pl.ds(pl.multiple_of(h * half, half), half)
    other = pl.ds(pl.multiple_of((1 - h) * half, half), half)
    copies = [
        pltpu.make_async_copy(grad.at[pl.ds(0, kept)], grad_out.at[pl.ds(0, kept)], sems.at[0]),
        pltpu.make_async_copy(adj.at[:, other], adj_out.at[:, other], sems.at[1]),
        pltpu.make_async_copy(grad_last, grad_out.at[last], sems.at[2]),
        pltpu.make_async_copy(adj_last, adj_out.at[:, cut], sems.at[3]),
    ]
    for copy in copies[:2]:
        copy.start()
    factor = jnp.max(discount_of(jnp.full((8, 128), section[0])))
    total = adj[:, cut] + lax.dot_general(
        t_own[last, :], c_all[k, last, :], (((0,), (0,)), ((), ())), preferred_element_type=jnp.float32
    )
    parts = decoded(p_in.at[h, p_in.shape[1] - 1])
    done = total.shape[0] - TILE
    adj_last[pl.ds(0, done), :] = factor * total[:done]
    tall = TILE // SHARE
    for i, part in enumerate(parts):
        top = done + i * tall
        adj_last[pl.ds(top, tall), :] = factor * (total[top : top + tall] + part)
    copies[3].start()
    grad_last[...] = factor * (
        grad[last, :]
        + lax.dot_general(
            c_all[k, last, :], v_all[k], (((1,), (1,)), ((), ())), preferred_element_type=jnp.float32
        )
    )
    copies[2].start()
    for copy in copies:
        copy.wait()


def exchanged(expected_cot, value_next, transition, section):
    states, cells = expected_cot.shape
    current, following = transition.shape
    dma = pltpu.SemaphoreType.DMA
    half = cells // 2
    tiles = following // TILE
    arrays = (expected_cot, value_next, transition)
    in_vmem = pl.BlockSpec(memory_space=pltpu.VMEM)
    in_hbm = pl.BlockSpec(memory_space=pltpu.HBM)
    in_smem = pl.BlockSpec(memory_space=pltpu.SMEM)
    outs = (
        jax.ShapeDtypeStruct((following, cells), jnp.float32),
        jax.ShapeDtypeStruct((current, following), jnp.float32),
    )
    held = (
        jax.ShapeDtypeStruct((8, states, half), jnp.bfloat16),
        jax.ShapeDtypeStruct((8, states, half), jnp.bfloat16),
        jax.ShapeDtypeStruct((current, following), jnp.bfloat16),
        jax.ShapeDtypeStruct((2, tiles, MESSAGE, half), jnp.int16),
    )
    sums = pl.pallas_call(
        kernel,
        out_shape=outs + held,
        in_specs=[in_smem] + [in_hbm] * 3,
        out_specs=(in_vmem,) * 6,
        scratch_shapes=[
            pltpu.VMEM((4, states, half), jnp.bfloat16),
            pltpu.VMEM((current, following), jnp.bfloat16),
            pltpu.VMEM((2, tiles, MESSAGE, half), jnp.int16),
            dma((8, PIECES)),
            dma((8, PIECES)),
            dma((8, PIECES)),
            dma((2, PIECES)),
            dma((4, PIECES)),
            dma((4,)),
            dma((4,)),
            dma((5,)),
            dma((5,)),
            dma((5,)),
            dma((2, tiles)),
            dma((2, tiles)),
        ],
        compiler_params=pltpu.CompilerParams(
            collective_id=0, has_side_effects=True, vmem_limit_bytes=VMEM_BYTES
        ),
    )(section, *(pltpu.with_memory_space_constraint(x, pltpu.HBM) for x in arrays))
    return pl.pallas_call(
        stored,
        out_shape=outs,
        in_specs=[in_smem] + [in_vmem] * 6,
        out_specs=(in_hbm,) * 2,
        scratch_shapes=[
            pltpu.VMEM((states // PIECES, following), jnp.float32),
            pltpu.VMEM((following, half), jnp.float32),
            dma((4,)),
        ],
        compiler_params=pltpu.CompilerParams(vmem_limit_bytes=STORE_BYTES),
    )(section, *(pltpu.with_memory_space_constraint(x, pltpu.VMEM) for x in sums))


def solution(mesh):
    shape = mesh.shape
    paired = shape["storage"] == 2 and shape["sub"] == 2 and shape["markov"] == 4
    body = exchanged if paired else gathered
    return jax.shard_map(
        body,
        mesh=mesh,
        in_specs=(
            P(("groups", "markov"), ("storage", "sub")),
            P(("groups", "markov"), ("storage", "sub")),
            P(("groups", "storage", "sub"), "markov"),
            P("groups"),
        ),
        out_specs=(
            P(("groups", "markov"), ("storage", "sub")),
            P(("groups", "storage", "sub"), "markov"),
        ),
        check_vma=False,
    )
```

```python
import jax
import jax.numpy as jnp
from jax import lax
from jax.experimental import pallas as pl
from jax.experimental.pallas import tpu as pltpu
from jax.sharding import PartitionSpec as P

discount_rate = 0.97
MESH = pl.DeviceIdType.MESH
PIECES = 4
TILE = 256
TALL = 512
STORE_BYTES = 6 * 1024 * 1024
AHEAD = 0
BITS = 20
BASE = 2 ** (BITS - 16)
SHARE = 16 // (BITS - 16)
MESSAGE = TILE + TILE // SHARE + 16
VMEM_BYTES = 30 * 1024 * 1024

PLAN = (
    ('v', 0, (0, 1, 4, 5)),
    ('own', 'u0', (2,)),
    ('wait', (-1, -1, -1, 2, -1, -1, -1, -1)),
    ('pair', 2, (3,)),
    ('own', 'f1', (6, 7)),
    ('v', 1, (0, 1, 4, 5)),
    ('own', 'u1', (2,)),
    ('wait', (-1, -1, -1, 3, -1, -1, -1, -1)),
    ('pair', 3, (3,)),
    ('own', 'f0', (6, 7)),
    ('wait', (2, -1, -1, -1, -1, -1, -1, -1)),
    ('pair', 2, (0,)),
    ('own', 'u0', (1,)),
    ('v', 1, (3, 6)),
    ('own', 'f0', (4, 5)),
    ('wait', (3, -1, -1, -1, -1, -1, -1, -1)),
    ('pair', 3, (0,)),
    ('own', 'u1', (1,)),
    ('v', 0, (3, 6)),
    ('own', 'f1', (4,)),
    ('wait', (-1, -1, -1, -1, -1, -1, 7, -1)),
    ('pair', 1, (6,)),
    ('hop', (82, -1, 87, 97, 86, 34, -1, 97)),
    ('hop', (114, -1, 119, 65, 118, 38, -1, 65)),
    ('v', 1, (2,)),
    ('hop', (90, -1, 82, 101, 82, 42, -1, 101)),
    ('wait', (-1, -1, -1, -1, -1, -1, -1, 2)),
    ('pair', 2, (7,)),
    ('hop', (122, -1, 95, 69, 94, 46, -1, 69)),
    ('pair', 2, (5,)),
    ('v', 1, (7,)),
    ('own', 'f1', (5,)),
    ('hop', (66, -1, 114, 105, 114, 50, -1, 105)),
    ('hop', (98, -1, 127, 73, 126, 54, -1, 73)),
    ('hop', (70, -1, 90, 109, 90, 97, -1, 109)),
    ('v', 0, (2,)),
    ('pair', 0, (3, 7)),
    ('wait', (-1, -1, -1, -1, -1, -1, -1, 3)),
    ('pair', 3, (7,)),
    ('hop', (102, -1, 122, -1, 122, 58, -1, 77)),
    ('pair', 1, (2, 4)),
    ('hop', (74, -1, 66, -1, 66, 65, -1, 113)),
    ('hop', (106, -1, 98, -1, 98, 62, -1, 81)),
    ('pair', 3, (5,)),
    ('hop', (78, -1, 70, -1, 70, 101, -1, 117)),
    ('hop', (110, -1, 102, -1, 102, 69, -1, 85)),
    ('pair', 0, (0,)),
    ('v', 0, (7,)),
    ('hop', (84, -1, 74, -1, 74, 105, -1, 121)),
    ('hop', (116, -1, 106, -1, 106, 73, -1, 89)),
    ('hop', (92, -1, 78, -1, 78, 109, -1, 124)),
    ('pair', 0, (5,)),
    ('pair', 1, (7,)),
    ('hop', (124, -1, 110, -1, 110, 77, -1, 92)),
    ('pair', 1, (0,)),
    ('pair', 0, (2, 4)),
    ('own', 'u0', (0,)),
    ('own', 'u1', (0,)),
    ('hop', (-1, -1, 34, -1, -1, 113, -1, -1)),
    ('hop', (-1, -1, 38, -1, -1, 81, -1, -1)),
    ('hop', (-1, -1, 42, -1, -1, 117, -1, -1)),
    ('hop', (-1, -1, 46, -1, -1, 85, -1, -1)),
    ('pair', 2, (2,)),
    ('hop', (-1, -1, 50, -1, -1, 127, -1, -1)),
    ('hop', (-1, -1, 54, -1, -1, 121, -1, -1)),
    ('pair', 1, (5,)),
    ('hop', (-1, -1, 58, -1, -1, 95, -1, -1)),
    ('hop', (-1, -1, 62, -1, -1, 89, -1, -1)),
    ('pair', 3, (2,)),
    ('wait', (-1, -1, -1, -1, -1, -1, 5, -1)),
    ('part', (-1, -1, -1, -1, 1, 1, 1, 1)),
    ('relay',),
    ('part', (-1, -1, -1, -1, 0, -1, -1, -1)),
    ('wait', (-1, 6, -1, -1, -1, -1, 6, -1)),
    ('pair', 0, (1, 6)),
    ('own', 'u0', (3,)),
    ('hop', (-1, -1, 2, 77, 34, -1, -1, -1)),
    ('hop', (-1, -1, 6, 113, 38, -1, -1, -1)),
    ('hop', (-1, -1, 10, 81, 42, -1, -1, -1)),
    ('own', 'd1', (2,)),
    ('hop', (-1, -1, 14, -1, -1, -1, -1, -1)),
    ('wait', (-1, 4, -1, -1, -1, -1, 4, -1)),
    ('part', (-1, 0, 0, 0, -1, 0, 0, -1)),
    ('hop', (-1, -1, -1, 117, -1, 2, -1, -1)),
    ('wait', (1, -1, -1, 1, -1, -1, -1, -1)),
    ('v_q', (1,)),
    ('grad', (1, 6, 5, 1, 5, 2, 5, 2)),
    ('hop', (-1, -1, 18, 85, 46, 6, -1, -1)),
    ('pair', 2, (4,)),
    ('hop', (-1, -1, 22, 125, -1, -1, -1, -1)),
    ('part', (0, -1, -1, -1, -1, -1, -1, 0)),
    ('hop', (-1, -1, 26, 121, 50, -1, -1, -1)),
    ('pair', 1, (3,)),
    ('v_q', (2, 4, 6)),
    ('grad', (2, 4, 7, 2, 7, 3, 7, 3)),
    ('hop', (-1, -1, 30, 93, -1, 10, -1, -1)),
    ('v_q', (5, 7)),
    ('grad', (3, -1, 4, 3, 4, 6, 4, 6)),
    ('hop', (-1, -1, -1, 89, 54, -1, -1, -1)),
    ('v_q', (3,)),
    ('grad', (4, -1, 6, 6, 6, 4, 6, 4)),
    ('wait', (-1, 3, -1, -1, -1, -1, -1, -1)),
    ('pair', 3, (1,)),
    ('wait', (-1, -1, -1, -1, -1, -1, 2, -1)),
    ('pair', 2, (6,)),
    ('hop', (-1, -1, -1, -1, 58, 14, -1, -1)),
    ('hop', (-1, -1, -1, -1, 62, -1, -1, -1)),
    ('pair', 3, (4,)),
    ('hop', (-1, -1, -1, -1, 2, -1, -1, -1)),
    ('v_q', (0,)),
    ('grad', (6, 3, 2, 4, 2, 7, 2, 7)),
    ('wait', (-1, 7, -1, -1, -1, -1, -1, -1)),
    ('pair', 1, (1,)),
    ('hop', (-1, -1, -1, -1, 6, -1, -1, -1)),
    ('grad', (5, 7, 3, 7, 3, 5, -1, 5)),
    ('wait', (-1, -1, -1, -1, -1, -1, 3, -1)),
    ('pair', 3, (6,)),
    ('hop', (-1, -1, -1, -1, 10, -1, -1, -1)),
    ('hop', (-1, -1, -1, -1, 14, -1, -1, -1)),
    ('wait', (-1, 5, -1, -1, -1, -1, -1, 0)),
    ('grad', (7, 5, 1, 5, 0, 0, -1, 0)),
    ('hop', (-1, -1, -1, -1, 18, -1, -1, -1)),
    ('part', (1, 1, 1, 1, -1, -1, -1, -1)),
    ('adj', (1, -1, 1, 1, 0, 0, -1, 0)),
    ('wait', (-1, 2, -1, -1, -1, -1, -1, -1)),
    ('pair', 2, (1,)),
    ('own', 'd0', (2,)),
    ('own', 'd1', (3,)),
    ('hop', (-1, -1, -1, -1, 22, -1, -1, -1)),
    ('hop', (-1, -1, -1, -1, 26, -1, -1, -1)),
    ('hop', (-1, -1, -1, -1, 30, -1, -1, -1)),
    ('grad', (-1, 2, -1, -1, -1, -1, 3, -1)),
    ('own', 'd0', (3,)),
    ('own', 'u1', (3,)),
    ('hop', (-1, -1, -1, -1, -1, 18, -1, -1)),
    ('hop', (-1, -1, -1, -1, -1, 22, -1, -1)),
    ('hop', (-1, -1, -1, -1, -1, 26, -1, -1)),
    ('hop', (-1, -1, -1, -1, -1, 30, -1, -1)),
    ('wait', (-1, 1, -1, -1, -1, -1, 0, -1)),
    ('adj', (-1, 1, -1, -1, -1, -1, 0, -1)),
    ('grad', (-1, 1, -1, -1, -1, -1, 0, -1)),
    ('pre', (0, 0, 0, 0, 1, 1, 1, 1)),
    ('fin', (0, 0, 0, 0, 1, 1, 1, 1), (0, 1, 3, 6, 7)),
)
CROSSING = (((0, 0, 0, 0), (0, 1, 0, 1)), ((3, 3, 3, 3), (3, 3, 3, 2)))


def discount_of(section):
    return jnp.exp(section.astype(jnp.float32) * jnp.log(jnp.float32(discount_rate)))


def gathered(expected_cot, value_next, transition, section):
    discount_factor = discount_of(section[0])
    cotangent_all = lax.all_gather(expected_cot, "markov", axis=0, tiled=True)
    adjoint_sum = lax.dot_general(
        lax.all_gather(transition, ("storage", "sub"), axis=0, tiled=True),
        cotangent_all,
        (((0,), (0,)), ((), ())),
        preferred_element_type=jnp.float32,
    )
    own_states = lax.all_to_all(
        cotangent_all, ("storage", "sub"), split_axis=0, concat_axis=1, tiled=True
    )
    gathered_values = lax.all_gather(value_next, ("storage", "sub"), axis=1, tiled=True)
    gradient_sum = lax.dot_general(
        own_states, gathered_values, (((1,), (1,)), ((), ())), preferred_element_type=jnp.float32
    )
    return (discount_factor * adjoint_sum, discount_factor * gradient_sum)


def pick(place, table):
    if len(set(table)) == 1:
        return table[0]
    value = table[0]
    for i, entry in enumerate(table[1:], 1):
        if entry != table[0]:
            value = jnp.where(place == i, entry, value)
    return value


def where(place, places, body):
    if len(places) == 8:
        body()
        return
    among = place == places[0]
    for i in places[1:]:
        among = among | (place == i)
    pl.when(among)(body)


def filled(table):
    return tuple(i for i, entry in enumerate(table) if entry >= 0)


def coded(value, out):
    top = jnp.maximum(jnp.max(jnp.abs(value), axis=0, keepdims=True), 2.0**-100)
    power = jnp.clip(jnp.ceil(jnp.log2(top * 1.0001)), -100, 100)
    whole = jnp.round(value * jnp.exp2(BITS - 1.0 - power)).astype(jnp.int32)
    low = whole & (BASE - 1)
    out[:TILE, :] = ((whole - low) >> (BITS - 16)).astype(jnp.int16)
    n = TILE // SHARE
    packed = low[:n] - 32768
    for i in range(1, SHARE):
        packed = packed + BASE**i * low[i * n : (i + 1) * n]
    out[TILE : TILE + n, :] = packed.astype(jnp.int16)
    out[TILE + n :, :] = jnp.broadcast_to(power.astype(jnp.int32), (16, value.shape[1])).astype(jnp.int16)


def decoded(message):
    n = TILE // SHARE
    high = message[:TILE, :].astype(jnp.int32) * BASE
    low = message[TILE : TILE + n, :].astype(jnp.int32) + 32768
    power = message[TILE + n :, :].astype(jnp.int32)[:1].astype(jnp.float32)
    unit = jnp.exp2(power - (BITS - 1.0))
    return [
        (high[i * n : (i + 1) * n] + ((low >> (BITS - 16) * i) & (BASE - 1))).astype(jnp.float32) * unit
        for i in range(SHARE)
    ]


def kernel(
    section, c_in, v_in, t_in, adj, grad, c_all, v_all, t_own, p_in, c_pair, t_pair, p_out,
    c_recv, up_send, down_send, own_send, own_extra, pair_send, pair_recv,
    v_send, v_recv, t_sems, p_send, p_recv,
):
    g, m = lax.axis_index("groups"), lax.axis_index("markov")
    s, u = lax.axis_index("storage"), lax.axis_index("sub")
    far = 1 - s
    j, p, o, q = 2 * s + u, 2 * s + 1 - u, 2 * far + u, 2 * far + 1 - u
    step = 1 - 2 * s
    z = m + s * (3 - 2 * m)
    row = u + s * (1 - 2 * u)
    place = 2 * z + row
    partner, across = (g, m, s, 1 - u), (g, m, far, u)
    home = lax.rem(m, 2)

    def column(to, side, core):
        return (g, jnp.clip(to, 0, 3), side, core)

    above, below = column(m + step, s, u), column(m - step, s, u)
    up_home, down_home = column(m + step, s, home), column(m - step, s, home)
    states, half = c_all.shape[1:]
    tall = states // PIECES
    following = grad.shape[1]
    is_a, is_b = (z <= 1) & (row == z), (z <= 1) & (row != z)
    pairs = [(h, r) for h in range(2) for r in range(PIECES)]

    def remote(src, dst, send, recv, to):
        return pltpu.make_async_remote_copy(
            src_ref=src, dst_ref=dst, send_sem=send, recv_sem=recv, device_id=to, device_id_type=MESH
        )

    def quarter(c):
        if isinstance(c, int):
            return (j, p, o, q)[c]
        return jnp.where(c == 0, j, jnp.where(c == 1, p, jnp.where(c == 2, o, q)))

    def chunk(code):
        return 2 * quarter(code // 2) + code % 2

    def held(k, r):
        return c_all.at[k, pl.ds(pl.multiple_of(r * tall, tall), tall)]

    def mine(h, r):
        return c_in.at[pl.ds(r * tall, tall), pl.ds(h * half, half)]

    def got(k, r):
        remote(held(k, r), held(k, r), c_recv.at[k, r], c_recv.at[k, r], partner).wait_recv()

    def z_copy(k, r, send, to):
        return remote(held(k, r), held(k, r), send, c_recv.at[k, r], to)

    def own_copy(h, r, send, to):
        return remote(mine(h, r), held(2 * j + h, r), send, c_recv.at[2 * j + h, r], to)

    def own_up(h, r):
        return own_copy(h, r, own_send.at[h, r], up_home)

    def own_down(h, r):
        return own_copy(h, r, own_extra.at[h, r], down_home)

    def own_far(h, r):
        at = jnp.where(z == 3, CROSSING[0][h][r], CROSSING[1][h][r])
        return own_copy(h, r, own_send.at[h, r], column(m + step * (3 - z - at), far, home))

    def own_ahead(h, r):
        return own_copy(h, r, own_extra.at[2 + h, r], column(m + 2 * step, s, home))

    def own_pair(h, r):
        return own_copy(h, r, own_extra.at[2 + h, r], partner)

    def pair_copy(i):
        k = (2 * q, 2 * q + 1, 2 * p, 2 * p + 1)[i]
        return remote(c_all.at[k], c_pair.at[i], pair_send.at[i], pair_recv.at[i], partner)

    def pair_got(i):
        remote(c_pair.at[i], c_pair.at[i], pair_recv.at[i], pair_recv.at[i], partner).wait_recv()

    def v_half(h):
        return v_in.at[:, pl.ds(h * half, half)]

    def v_across(h):
        return remote(v_half(h), v_all.at[2 * j + h], v_send.at[h], v_recv.at[h], across)

    def v_relay():
        part = v_all.at[pl.ds(2 * o, 2)]
        return remote(part, part, v_send.at[2], v_recv.at[2], partner)

    def v_pair(h):
        return remote(v_half(h), v_all.at[2 * j + h], v_send.at[3 + h], v_recv.at[3 + h], partner)

    def t_copy():
        return remote(t_in, t_pair, t_sems.at[0], t_sems.at[1], partner)

    def p_copy(h, n):
        return remote(p_out.at[h, n], p_in.at[h, n], p_send.at[h, n], p_recv.at[h, n], across)

    barrier = pltpu.get_barrier_semaphore()
    for dz in range(4):
        for dc in range(4):
            if dz or dc:
                to = (g, lax.rem(m + dz, 4), lax.rem(s + dc // 2, 2), lax.rem(u + dc % 2, 2))
                pl.semaphore_signal(barrier, inc=1, device_id=to, device_id_type=MESH)

    locals_ = [pltpu.make_async_copy(t_in, t_own, t_sems.at[2])]
    for h in range(2):
        locals_.append(pltpu.make_async_copy(v_half(h), v_all.at[2 * j + h], t_sems.at[3 + h]))

    @pl.when(is_a)
    def _():
        for h, r in pairs:
            pltpu.make_async_copy(mine(h, r), held(2 * j + h, r), c_recv.at[2 * j + h, r]).start()

    for copy in locals_:
        copy.start()
    pl.semaphore_wait(barrier, 15)

    def hop(table):
        def body():
            code = pick(place, tuple(entry // 4 for entry in table))
            k, r = chunk(code // PIECES), code % PIECES
            got(k, r)
            ups = tuple(i for i in filled(table) if table[i] % 4 >= 2)
            downs = tuple(i for i in filled(table) if table[i] % 2)
            if ups:
                where(place, ups, lambda: z_copy(k, r, up_send, above).start())
            if downs:
                where(place, downs, lambda: z_copy(k, r, down_send, below).start())

        where(place, filled(table), body)

    def bulk(table):
        def body():
            k = chunk(pick(place, table))
            for r in range(PIECES):
                got(k, r)

        where(place, filled(table), body)

    def own(name, places):
        copy, h = {"u": own_up, "d": own_down, "f": own_far, "x": own_ahead}[name[0]], int(name[1])

        def body():
            for r in range(AHEAD if name[0] == "x" else PIECES):
                copy(h, r).start()

        where(place, places, body)

    def both(t_block, at, c_block):
        return lax.dot_general(
            t_block[:, at], c_block[...], (((0,), (0,)), ((), ())), preferred_element_type=jnp.float32
        )

    def part(table):
        def body():
            h = pick(place, table)
            pair_got(h)

            @pl.loop(0, following // TILE)
            def _(n):
                at = pl.ds(pl.multiple_of(n * TILE, TILE), TILE)
                value = both(t_own, at, c_all.at[2 * o + h]) + both(t_pair, at, c_pair.at[h])
                coded(value, p_out.at[h, n])
                p_copy(h, n).start()

        where(place, filled(table), body)

    def adjoint(table, factor):
        def body():
            h = pick(place, table)
            pair_got(2 + h)
            cut = pl.ds(pl.multiple_of(h * half, half), half)

            @pl.loop(0, following // TILE)
            def _(n):
                at = pl.ds(pl.multiple_of(n * TILE, TILE), TILE)
                value = both(t_own, at, c_all.at[2 * j + h]) + both(t_pair, at, c_pair.at[2 + h])
                p_copy(h, n).wait_recv()
                tall = TILE // SHARE
                for i, part in enumerate(decoded(p_in.at[h, n])):
                    rows = pl.ds(pl.multiple_of(n * TILE + i * tall, tall), tall)
                    adj[rows, cut] = factor * (value[i * tall : (i + 1) * tall] + part)

        where(place, filled(table), body)

    def product(k, at):
        return lax.dot_general(
            c_all[k, at, :], v_all[k], (((1,), (1,)), ((), ())), preferred_element_type=jnp.float32
        )

    def gradient(table, first):
        def body():
            k = chunk(pick(place, table))

            @pl.loop(0, states // TALL)
            def _(n):
                at = pl.ds(pl.multiple_of(n * TALL, TALL), TALL)
                grad[at, :] = product(k, at) if first else grad[at, :] + product(k, at)

        where(place, filled(table), body)

    tiles = following // TILE

    def cut_of(h):
        return pl.ds(pl.multiple_of(h * half, half), half)

    def add_partial(h, n):
        p_copy(h, n).wait_recv()
        top = TILE // SHARE
        for i, value in enumerate(decoded(p_in.at[h, n])):
            at = pl.ds(n * TILE + i * top, top)
            adj[at, cut_of(h)] += value

    def begin(table):
        h = pick(place, table)
        pair_got(2 + h)

        @pl.loop(0, tiles)
        def _(n):
            at = pl.ds(pl.multiple_of(n * TILE, TILE), TILE)
            adj[at, cut_of(h)] = both(t_pair, at, c_pair.at[2 + h])

        for n in range(tiles - 1):
            add_partial(h, n)

    def finish(table, late, factor):
        h = pick(place, table)
        k = 2 * j + h
        late_got = lambda r: where(place, late, lambda: got(k, r)) if late else None

        @pl.loop(0, PIECES - 1)
        def _(r):
            late_got(r)
            at = pl.ds(pl.multiple_of(r * tall, tall), tall)
            grad[at, :] = factor * (grad[at, :] + product(k, at))
            adj[:, cut_of(h)] += lax.dot_general(
                t_own[at, :], c_all[k, at, :], (((0,), (0,)), ((), ())),
                preferred_element_type=jnp.float32,
            )

        late_got(PIECES - 1)
        p_copy(h, tiles - 1).wait_recv()

    def sent(send, bit):
        counts = [0] * 8
        for kind, *rest in PLAN:
            if kind == "hop":
                for i, entry in enumerate(rest[0]):
                    counts[i] += int(entry >= 0 and entry // bit % 2 == 1)
        rows = tall * half * 2 // (following * 4)
        for count in sorted(set(counts) - {0}):
            part = grad.at[pl.ds(0, count * rows)]
            places = tuple(i for i in range(8) if counts[i] == count)
            where(place, places, lambda: remote(part, part, send, send, partner).wait_send())

    def drain():
        for h, r in pairs:
            own_up(h, r).wait_send()

            @pl.when((z == 1))
            def _():
                own_down(h, r).wait_send()

            @pl.when(is_b)
            def _():
                own_pair(h, r).wait_send()

        for r in range(AHEAD):
            pl.when(is_a & (z == 1))(lambda: own_ahead(0, r).wait_send())

        sent(down_send, 1)
        for i in range(4):
            pair_copy(i).wait_send()
        for h in range(2):
            v_across(h).wait_send()
            v_pair(h).wait_send()
        v_relay().wait_send()
        t_copy().wait_send()

    def begin_pairs():
        @pl.when(is_b)
        def _():
            for h, r in pairs:
                own_pair(h, r).start()

        t_copy().start()
        for h in range(2):
            v_pair(h).start()

    begun, ready, graded = False, False, False
    for kind, *rest in PLAN:
        if kind not in ("own", "v") and not begun:
            begun = True
            begin_pairs()
        if kind in ("part", "grad") and not ready:
            ready = True
            factor = jnp.max(discount_of(jnp.full((8, 128), section[0])))
            for copy in locals_:
                copy.wait()
            t_copy().wait_recv()
            for h in range(2):
                v_pair(h).wait_recv()
        if kind == "hop":
            hop(*rest)
        elif kind == "wait":
            bulk(*rest)
        elif kind == "own":
            own(*rest)
        elif kind == "v":
            where(place, rest[1], lambda: v_across(rest[0]).start())
        elif kind == "pair":
            where(place, rest[1], lambda: pair_copy(rest[0]).start())
        elif kind == "part":
            part(*rest)
        elif kind == "relay":
            for h in range(2):
                v_across(h).wait_recv()
            v_relay().start()
        elif kind == "v_q":
            where(place, rest[0], lambda: v_relay().wait_recv())
        elif kind == "grad":
            gradient(*rest, not graded)
            graded = True
        elif kind == "adj":
            adjoint(*rest, factor)
        elif kind == "pre":
            begin(*rest)
        else:
            drain()
            finish(*rest, factor)
            sent(up_send, 2)

    for h in range(2):
        for n in range(following // TILE):
            p_copy(h, n).wait_send()


def stored(section, adj, grad, c_all, v_all, t_own, p_in, adj_out, grad_out, grad_last, adj_last, sems):
    m, s, u = (lax.axis_index(name) for name in ("markov", "storage", "sub"))
    place = 2 * (m + s * (3 - 2 * m)) + u + s * (1 - 2 * u)
    h = pick(place, PLAN[-1][1])
    k = 2 * (2 * s + u) + h
    states, half = c_all.shape[1:]
    kept = states - states // PIECES
    last = pl.ds(kept, states - kept)
    cut = pl.ds(pl.multiple_of(h * half, half), half)
    other = pl.ds(pl.multiple_of((1 - h) * half, half), half)
    copies = [
        pltpu.make_async_copy(grad.at[pl.ds(0, kept)], grad_out.at[pl.ds(0, kept)], sems.at[0]),
        pltpu.make_async_copy(adj.at[:, other], adj_out.at[:, other], sems.at[1]),
        pltpu.make_async_copy(grad_last, grad_out.at[last], sems.at[2]),
        pltpu.make_async_copy(adj_last, adj_out.at[:, cut], sems.at[3]),
    ]
    for copy in copies[:2]:
        copy.start()
    factor = jnp.max(discount_of(jnp.full((8, 128), section[0])))
    total = adj[:, cut] + lax.dot_general(
        t_own[last, :], c_all[k, last, :], (((0,), (0,)), ((), ())), preferred_element_type=jnp.float32
    )
    parts = decoded(p_in.at[h, p_in.shape[1] - 1])
    done = total.shape[0] - TILE
    adj_last[pl.ds(0, done), :] = factor * total[:done]
    tall = TILE // SHARE
    for i, part in enumerate(parts):
        top = done + i * tall
        adj_last[pl.ds(top, tall), :] = factor * (total[top : top + tall] + part)
    copies[3].start()
    grad_last[...] = factor * (
        grad[last, :]
        + lax.dot_general(
            c_all[k, last, :], v_all[k], (((1,), (1,)), ((), ())), preferred_element_type=jnp.float32
        )
    )
    copies[2].start()
    for copy in copies:
        copy.wait()


def exchanged(expected_cot, value_next, transition, section):
    states, cells = expected_cot.shape
    current, following = transition.shape
    dma = pltpu.SemaphoreType.DMA
    half = cells // 2
    tiles = following // TILE
    arrays = (expected_cot, value_next, transition)
    in_vmem = pl.BlockSpec(memory_space=pltpu.VMEM)
    in_hbm = pl.BlockSpec(memory_space=pltpu.HBM)
    in_smem = pl.BlockSpec(memory_space=pltpu.SMEM)
    outs = (
        jax.ShapeDtypeStruct((following, cells), jnp.float32),
        jax.ShapeDtypeStruct((current, following), jnp.float32),
    )
    held = (
        jax.ShapeDtypeStruct((8, states, half), jnp.bfloat16),
        jax.ShapeDtypeStruct((8, states, half), jnp.bfloat16),
        jax.ShapeDtypeStruct((current, following), jnp.bfloat16),
        jax.ShapeDtypeStruct((2, tiles, MESSAGE, half), jnp.int16),
    )
    sums = pl.pallas_call(
        kernel,
        out_shape=outs + held,
        in_specs=[in_smem] + [in_hbm] * 3,
        out_specs=(in_vmem,) * 6,
        scratch_shapes=[
            pltpu.VMEM((4, states, half), jnp.bfloat16),
            pltpu.VMEM((current, following), jnp.bfloat16),
            pltpu.VMEM((2, tiles, MESSAGE, half), jnp.int16),
            dma((8, PIECES)),
            dma,
            dma,
            dma((2, PIECES)),
            dma((4, PIECES)),
            dma((4,)),
            dma((4,)),
            dma((5,)),
            dma((5,)),
            dma((5,)),
            dma((2, tiles)),
            dma((2, tiles)),
        ],
        compiler_params=pltpu.CompilerParams(
            collective_id=0, has_side_effects=True, vmem_limit_bytes=VMEM_BYTES
        ),
    )(section, *(pltpu.with_memory_space_constraint(x, pltpu.HBM) for x in arrays))
    return pl.pallas_call(
        stored,
        out_shape=outs,
        in_specs=[in_smem] + [in_vmem] * 6,
        out_specs=(in_hbm,) * 2,
        scratch_shapes=[
            pltpu.VMEM((states // PIECES, following), jnp.float32),
            pltpu.VMEM((following, half), jnp.float32),
            dma((4,)),
        ],
        compiler_params=pltpu.CompilerParams(vmem_limit_bytes=STORE_BYTES),
    )(section, *(pltpu.with_memory_space_constraint(x, pltpu.VMEM) for x in sums))


def solution(mesh):
    shape = mesh.shape
    paired = shape["storage"] == 2 and shape["sub"] == 2 and shape["markov"] == 4
    body = exchanged if paired else gathered
    return jax.shard_map(
        body,
        mesh=mesh,
        in_specs=(
            P(("groups", "markov"), ("storage", "sub")),
            P(("groups", "markov"), ("storage", "sub")),
            P(("groups", "storage", "sub"), "markov"),
            P("groups"),
        ),
        out_specs=(
            P(("groups", "markov"), ("storage", "sub")),
            P(("groups", "storage", "sub"), "markov"),
        ),
        check_vma=False,
    )
```

```python
import jax
import jax.numpy as jnp
from jax import lax
from jax.experimental import pallas as pl
from jax.experimental.pallas import tpu as pltpu
from jax.sharding import PartitionSpec as P

discount_rate = 0.97
MESH = pl.DeviceIdType.MESH
PIECES = 4
TILE = 256
TALL = 512
STORE_BYTES = 6 * 1024 * 1024
AHEAD = 0
BITS = 20
BASE = 2 ** (BITS - 16)
SHARE = 16 // (BITS - 16)
MESSAGE = TILE + TILE // SHARE + 16
VMEM_BYTES = 30 * 1024 * 1024

PLAN = (
    ('v', 0, (0, 1, 4, 5)),
    ('own', 'u0', (2,)),
    ('wait', (-1, -1, -1, 2, -1, -1, -1, -1)),
    ('pair', 2, (3,)),
    ('own', 'f1', (6, 7)),
    ('v', 1, (0, 1, 4, 5)),
    ('own', 'u1', (2,)),
    ('wait', (-1, -1, -1, 3, -1, -1, -1, -1)),
    ('pair', 3, (3,)),
    ('own', 'f0', (6, 7)),
    ('wait', (2, -1, -1, -1, -1, -1, -1, -1)),
    ('pair', 2, (0,)),
    ('own', 'u0', (1,)),
    ('v', 1, (3, 6)),
    ('own', 'f0', (4, 5)),
    ('wait', (3, -1, -1, -1, -1, -1, -1, -1)),
    ('pair', 3, (0,)),
    ('own', 'u1', (1,)),
    ('v', 0, (3, 6)),
    ('own', 'f1', (4,)),
    ('wait', (-1, -1, -1, -1, -1, -1, 7, -1)),
    ('pair', 1, (6,)),
    ('hop', (82, -1, 87, 97, 86, 34, -1, 97)),
    ('hop', (114, -1, 119, 65, 118, 38, -1, 65)),
    ('v', 1, (2,)),
    ('hop', (90, -1, 82, 101, 82, 42, -1, 101)),
    ('wait', (-1, -1, -1, -1, -1, -1, -1, 2)),
    ('pair', 2, (7,)),
    ('hop', (122, -1, 95, 69, 94, 46, -1, 69)),
    ('pair', 2, (5,)),
    ('v', 1, (7,)),
    ('own', 'f1', (5,)),
    ('hop', (66, -1, 114, 105, 114, 50, -1, 105)),
    ('hop', (98, -1, 127, 73, 126, 54, -1, 73)),
    ('hop', (70, -1, 90, 109, 90, 97, -1, 109)),
    ('v', 0, (2,)),
    ('pair', 0, (3, 7)),
    ('wait', (-1, -1, -1, -1, -1, -1, -1, 3)),
    ('pair', 3, (7,)),
    ('hop', (102, -1, 122, -1, 122, 58, -1, 77)),
    ('pair', 1, (2, 4)),
    ('hop', (74, -1, 66, -1, 66, 65, -1, 113)),
    ('hop', (106, -1, 98, -1, 98, 62, -1, 81)),
    ('pair', 3, (5,)),
    ('hop', (78, -1, 70, -1, 70, 101, -1, 117)),
    ('hop', (110, -1, 102, -1, 102, 69, -1, 85)),
    ('pair', 0, (0,)),
    ('v', 0, (7,)),
    ('hop', (84, -1, 74, -1, 74, 105, -1, 121)),
    ('hop', (116, -1, 106, -1, 106, 73, -1, 89)),
    ('hop', (92, -1, 78, -1, 78, 109, -1, 124)),
    ('pair', 0, (5,)),
    ('pair', 1, (7,)),
    ('hop', (124, -1, 110, -1, 110, 77, -1, 92)),
    ('pair', 1, (0,)),
    ('pair', 0, (2, 4)),
    ('own', 'u0', (0,)),
    ('own', 'u1', (0,)),
    ('hop', (-1, -1, 34, -1, -1, 113, -1, -1)),
    ('hop', (-1, -1, 38, -1, -1, 81, -1, -1)),
    ('hop', (-1, -1, 42, -1, -1, 117, -1, -1)),
    ('hop', (-1, -1, 46, -1, -1, 85, -1, -1)),
    ('pair', 2, (2,)),
    ('hop', (-1, -1, 50, -1, -1, 127, -1, -1)),
    ('hop', (-1, -1, 54, -1, -1, 121, -1, -1)),
    ('pair', 1, (5,)),
    ('hop', (-1, -1, 58, -1, -1, 95, -1, -1)),
    ('hop', (-1, -1, 62, -1, -1, 89, -1, -1)),
    ('pair', 3, (2,)),
    ('wait', (-1, -1, -1, -1, -1, -1, 5, -1)),
    ('part', (-1, -1, -1, -1, 1, 1, 1, 1)),
    ('relay',),
    ('part', (-1, -1, -1, -1, 0, -1, -1, -1)),
    ('wait', (-1, 6, -1, -1, -1, -1, 6, -1)),
    ('pair', 0, (1, 6)),
    ('own', 'u0', (3,)),
    ('hop', (-1, -1, 2, 77, 34, -1, -1, -1)),
    ('hop', (-1, -1, 6, 113, 38, -1, -1, -1)),
    ('hop', (-1, -1, 10, 81, 42, -1, -1, -1)),
    ('own', 'd1', (2,)),
    ('hop', (-1, -1, 14, -1, -1, -1, -1, -1)),
    ('wait', (-1, 4, -1, -1, -1, -1, 4, -1)),
    ('part', (-1, 0, 0, 0, -1, 0, 0, -1)),
    ('hop', (-1, -1, -1, 117, -1, 2, -1, -1)),
    ('wait', (1, -1, -1, 1, -1, -1, -1, -1)),
    ('v_q', (1,)),
    ('grad', (1, 6, 5, 1, 5, 2, 5, 2)),
    ('hop', (-1, -1, 18, 85, 46, 6, -1, -1)),
    ('pair', 2, (4,)),
    ('hop', (-1, -1, 22, 125, -1, -1, -1, -1)),
    ('part', (0, -1, -1, -1, -1, -1, -1, 0)),
    ('hop', (-1, -1, 26, 121, 50, -1, -1, -1)),
    ('pair', 1, (3,)),
    ('v_q', (2, 4, 6)),
    ('grad', (2, 4, 7, 2, 7, 3, 7, 3)),
    ('hop', (-1, -1, 30, 93, -1, 10, -1, -1)),
    ('v_q', (5, 7)),
    ('grad', (3, -1, 4, 3, 4, 6, 4, 6)),
    ('hop', (-1, -1, -1, 89, 54, -1, -1, -1)),
    ('v_q', (3,)),
    ('grad', (4, -1, 6, 6, 6, 4, 6, 4)),
    ('wait', (-1, 3, -1, -1, -1, -1, -1, -1)),
    ('pair', 3, (1,)),
    ('wait', (-1, -1, -1, -1, -1, -1, 2, -1)),
    ('pair', 2, (6,)),
    ('hop', (-1, -1, -1, -1, 58, 14, -1, -1)),
    ('hop', (-1, -1, -1, -1, 62, -1, -1, -1)),
    ('pair', 3, (4,)),
    ('hop', (-1, -1, -1, -1, 2, -1, -1, -1)),
    ('v_q', (0,)),
    ('grad', (6, 3, 2, 4, 2, 7, 2, 7)),
    ('wait', (-1, 7, -1, -1, -1, -1, -1, -1)),
    ('pair', 1, (1,)),
    ('hop', (-1, -1, -1, -1, 6, -1, -1, -1)),
    ('grad', (5, 7, 3, 7, 3, 5, -1, 5)),
    ('wait', (-1, -1, -1, -1, -1, -1, 3, -1)),
    ('pair', 3, (6,)),
    ('hop', (-1, -1, -1, -1, 10, -1, -1, -1)),
    ('hop', (-1, -1, -1, -1, 14, -1, -1, -1)),
    ('wait', (-1, 5, -1, -1, -1, -1, -1, 0)),
    ('grad', (7, 5, 1, 5, 0, 0, -1, 0)),
    ('hop', (-1, -1, -1, -1, 18, -1, -1, -1)),
    ('part', (1, 1, 1, 1, -1, -1, -1, -1)),
    ('adj', (1, -1, 1, 1, 0, 0, -1, 0)),
    ('wait', (-1, 2, -1, -1, -1, -1, -1, -1)),
    ('pair', 2, (1,)),
    ('own', 'd0', (2,)),
    ('own', 'd1', (3,)),
    ('hop', (-1, -1, -1, -1, 22, -1, -1, -1)),
    ('hop', (-1, -1, -1, -1, 26, -1, -1, -1)),
    ('hop', (-1, -1, -1, -1, 30, -1, -1, -1)),
    ('grad', (-1, 2, -1, -1, -1, -1, 3, -1)),
    ('own', 'd0', (3,)),
    ('own', 'u1', (3,)),
    ('hop', (-1, -1, -1, -1, -1, 18, -1, -1)),
    ('hop', (-1, -1, -1, -1, -1, 22, -1, -1)),
    ('hop', (-1, -1, -1, -1, -1, 26, -1, -1)),
    ('hop', (-1, -1, -1, -1, -1, 30, -1, -1)),
    ('wait', (-1, 1, -1, -1, -1, -1, 0, -1)),
    ('adj', (-1, 1, -1, -1, -1, -1, 0, -1)),
    ('grad', (-1, 1, -1, -1, -1, -1, 0, -1)),
    ('pre', (0, 0, 0, 0, 1, 1, 1, 1)),
    ('fin', (0, 0, 0, 0, 1, 1, 1, 1), (0, 1, 3, 6, 7)),
)
CROSSING = (((0, 0, 0, 0), (0, 1, 0, 1)), ((3, 3, 3, 3), (3, 3, 3, 2)))


def discount_of(section):
    return jnp.exp(section.astype(jnp.float32) * jnp.log(jnp.float32(discount_rate)))


def gathered(expected_cot, value_next, transition, section):
    discount_factor = discount_of(section[0])
    cotangent_all = lax.all_gather(expected_cot, "markov", axis=0, tiled=True)
    adjoint_sum = lax.dot_general(
        lax.all_gather(transition, ("storage", "sub"), axis=0, tiled=True),
        cotangent_all,
        (((0,), (0,)), ((), ())),
        preferred_element_type=jnp.float32,
    )
    own_states = lax.all_to_all(
        cotangent_all, ("storage", "sub"), split_axis=0, concat_axis=1, tiled=True
    )
    gathered_values = lax.all_gather(value_next, ("storage", "sub"), axis=1, tiled=True)
    gradient_sum = lax.dot_general(
        own_states, gathered_values, (((1,), (1,)), ((), ())), preferred_element_type=jnp.float32
    )
    return (discount_factor * adjoint_sum, discount_factor * gradient_sum)


def pick(place, table):
    if len(set(table)) == 1:
        return table[0]
    value = table[0]
    for i, entry in enumerate(table[1:], 1):
        if entry != table[0]:
            value = jnp.where(place == i, entry, value)
    return value


def where(place, places, body):
    if len(places) == 8:
        body()
        return
    among = place == places[0]
    for i in places[1:]:
        among = among | (place == i)
    pl.when(among)(body)


def filled(table):
    return tuple(i for i, entry in enumerate(table) if entry >= 0)


def coded(value, out):
    top = jnp.maximum(jnp.max(jnp.abs(value), axis=0, keepdims=True), 2.0**-100)
    power = jnp.clip(jnp.ceil(jnp.log2(top * 1.0001)), -100, 100)
    whole = jnp.round(value * jnp.exp2(BITS - 1.0 - power)).astype(jnp.int32)
    low = whole & (BASE - 1)
    out[:TILE, :] = ((whole - low) >> (BITS - 16)).astype(jnp.int16)
    n = TILE // SHARE
    packed = low[:n] - 32768
    for i in range(1, SHARE):
        packed = packed + BASE**i * low[i * n : (i + 1) * n]
    out[TILE : TILE + n, :] = packed.astype(jnp.int16)
    out[TILE + n :, :] = jnp.broadcast_to(power.astype(jnp.int32), (16, value.shape[1])).astype(jnp.int16)


def decoded(message):
    n = TILE // SHARE
    high = message[:TILE, :].astype(jnp.int32) * BASE
    low = message[TILE : TILE + n, :].astype(jnp.int32) + 32768
    power = message[TILE + n :, :].astype(jnp.int32)[:1].astype(jnp.float32)
    unit = jnp.exp2(power - (BITS - 1.0))
    return [
        (high[i * n : (i + 1) * n] + ((low >> (BITS - 16) * i) & (BASE - 1))).astype(jnp.float32) * unit
        for i in range(SHARE)
    ]


def kernel(
    section, c_in, v_in, t_in, adj, grad, c_all, v_all, t_own, p_in, c_pair, t_pair, p_out,
    c_recv, up_send, down_send, own_send, own_extra, pair_send, pair_recv,
    v_send, v_recv, t_sems, p_send, p_recv,
):
    g, m = lax.axis_index("groups"), lax.axis_index("markov")
    s, u = lax.axis_index("storage"), lax.axis_index("sub")
    far = 1 - s
    j, p, o, q = 2 * s + u, 2 * s + 1 - u, 2 * far + u, 2 * far + 1 - u
    step = 1 - 2 * s
    z = m + s * (3 - 2 * m)
    row = u + s * (1 - 2 * u)
    place = 2 * z + row
    partner, across = (g, m, s, 1 - u), (g, m, far, u)
    home = lax.rem(m, 2)

    def column(to, side, core):
        return (g, jnp.clip(to, 0, 3), side, core)

    above, below = column(m + step, s, u), column(m - step, s, u)
    up_home, down_home = column(m + step, s, home), column(m - step, s, home)
    states, half = c_all.shape[1:]
    tall = states // PIECES
    following = grad.shape[1]
    is_a, is_b = (z <= 1) & (row == z), (z <= 1) & (row != z)
    pairs = [(h, r) for h in range(2) for r in range(PIECES)]

    def remote(src, dst, send, recv, to):
        return pltpu.make_async_remote_copy(
            src_ref=src, dst_ref=dst, send_sem=send, recv_sem=recv, device_id=to, device_id_type=MESH
        )

    def quarter(c):
        if isinstance(c, int):
            return (j, p, o, q)[c]
        return jnp.where(c == 0, j, jnp.where(c == 1, p, jnp.where(c == 2, o, q)))

    def chunk(code):
        return 2 * quarter(code // 2) + code % 2

    def held(k, r):
        return c_all.at[k, pl.ds(pl.multiple_of(r * tall, tall), tall)]

    def mine(h, r):
        return c_in.at[pl.ds(r * tall, tall), pl.ds(h * half, half)]

    def got(k, r):
        remote(held(k, r), held(k, r), c_recv.at[k, r], c_recv.at[k, r], partner).wait_recv()

    def z_copy(k, r, send, to):
        return remote(held(k, r), held(k, r), send, c_recv.at[k, r], to)

    def own_copy(h, r, send, to):
        return remote(mine(h, r), held(2 * j + h, r), send, c_recv.at[2 * j + h, r], to)

    def own_up(h, r):
        return own_copy(h, r, own_send, up_home)

    def own_down(h, r):
        return own_copy(h, r, own_extra.at[0], down_home)

    def own_far(h, r):
        at = jnp.where(z == 3, CROSSING[0][h][r], CROSSING[1][h][r])
        return own_copy(h, r, own_send, column(m + step * (3 - z - at), far, home))

    def own_ahead(h, r):
        return own_copy(h, r, own_extra.at[2], column(m + 2 * step, s, home))

    def own_pair(h, r):
        return own_copy(h, r, own_extra.at[1], partner)

    def pair_copy(i):
        k = (2 * q, 2 * q + 1, 2 * p, 2 * p + 1)[i]
        return remote(c_all.at[k], c_pair.at[i], pair_send.at[i], pair_recv.at[i], partner)

    def pair_got(i):
        remote(c_pair.at[i], c_pair.at[i], pair_recv.at[i], pair_recv.at[i], partner).wait_recv()

    def v_half(h):
        return v_in.at[:, pl.ds(h * half, half)]

    def v_across(h):
        return remote(v_half(h), v_all.at[2 * j + h], v_send.at[h], v_recv.at[h], across)

    def v_relay():
        part = v_all.at[pl.ds(2 * o, 2)]
        return remote(part, part, v_send.at[2], v_recv.at[2], partner)

    def v_pair(h):
        return remote(v_half(h), v_all.at[2 * j + h], v_send.at[3 + h], v_recv.at[3 + h], partner)

    def t_copy():
        return remote(t_in, t_pair, t_sems.at[0], t_sems.at[1], partner)

    def p_copy(h, n):
        return remote(p_out.at[h, n], p_in.at[h, n], p_send, p_recv.at[h, n], across)

    barrier = pltpu.get_barrier_semaphore()
    for dz in range(4):
        for dc in range(4):
            if dz or dc:
                to = (g, lax.rem(m + dz, 4), lax.rem(s + dc // 2, 2), lax.rem(u + dc % 2, 2))
                pl.semaphore_signal(barrier, inc=1, device_id=to, device_id_type=MESH)

    locals_ = [pltpu.make_async_copy(t_in, t_own, t_sems.at[2])]
    for h in range(2):
        locals_.append(pltpu.make_async_copy(v_half(h), v_all.at[2 * j + h], t_sems.at[3 + h]))

    @pl.when(is_a)
    def _():
        for h, r in pairs:
            pltpu.make_async_copy(mine(h, r), held(2 * j + h, r), c_recv.at[2 * j + h, r]).start()

    for copy in locals_:
        copy.start()
    pl.semaphore_wait(barrier, 15)

    def hop(table):
        def body():
            code = pick(place, tuple(entry // 4 for entry in table))
            k, r = chunk(code // PIECES), code % PIECES
            got(k, r)
            ups = tuple(i for i in filled(table) if table[i] % 4 >= 2)
            downs = tuple(i for i in filled(table) if table[i] % 2)
            if ups:
                where(place, ups, lambda: z_copy(k, r, up_send, above).start())
            if downs:
                where(place, downs, lambda: z_copy(k, r, down_send, below).start())

        where(place, filled(table), body)

    def bulk(table):
        def body():
            k = chunk(pick(place, table))
            for r in range(PIECES):
                got(k, r)

        where(place, filled(table), body)

    def own(name, places):
        copy, h = {"u": own_up, "d": own_down, "f": own_far, "x": own_ahead}[name[0]], int(name[1])

        def body():
            for r in range(AHEAD if name[0] == "x" else PIECES):
                copy(h, r).start()

        where(place, places, body)

    def both(t_block, at, c_block):
        return lax.dot_general(
            t_block[:, at], c_block[...], (((0,), (0,)), ((), ())), preferred_element_type=jnp.float32
        )

    def part(table):
        def body():
            h = pick(place, table)
            pair_got(h)

            @pl.loop(0, following // TILE)
            def _(n):
                at = pl.ds(pl.multiple_of(n * TILE, TILE), TILE)
                value = both(t_own, at, c_all.at[2 * o + h]) + both(t_pair, at, c_pair.at[h])
                coded(value, p_out.at[h, n])
                p_copy(h, n).start()

        where(place, filled(table), body)

    def adjoint(table, factor):
        def body():
            h = pick(place, table)
            pair_got(2 + h)
            cut = pl.ds(pl.multiple_of(h * half, half), half)

            @pl.loop(0, following // TILE)
            def _(n):
                at = pl.ds(pl.multiple_of(n * TILE, TILE), TILE)
                value = both(t_own, at, c_all.at[2 * j + h]) + both(t_pair, at, c_pair.at[2 + h])
                p_copy(h, n).wait_recv()
                tall = TILE // SHARE
                for i, part in enumerate(decoded(p_in.at[h, n])):
                    rows = pl.ds(pl.multiple_of(n * TILE + i * tall, tall), tall)
                    adj[rows, cut] = factor * (value[i * tall : (i + 1) * tall] + part)

        where(place, filled(table), body)

    def product(k, at):
        return lax.dot_general(
            c_all[k, at, :], v_all[k], (((1,), (1,)), ((), ())), preferred_element_type=jnp.float32
        )

    def gradient(table, first):
        def body():
            k = chunk(pick(place, table))

            @pl.loop(0, states // TALL)
            def _(n):
                at = pl.ds(pl.multiple_of(n * TALL, TALL), TALL)
                grad[at, :] = product(k, at) if first else grad[at, :] + product(k, at)

        where(place, filled(table), body)

    tiles = following // TILE

    def cut_of(h):
        return pl.ds(pl.multiple_of(h * half, half), half)

    def add_partial(h, n):
        p_copy(h, n).wait_recv()
        top = TILE // SHARE
        for i, value in enumerate(decoded(p_in.at[h, n])):
            at = pl.ds(n * TILE + i * top, top)
            adj[at, cut_of(h)] += value

    def begin(table):
        h = pick(place, table)
        pair_got(2 + h)

        @pl.loop(0, tiles)
        def _(n):
            at = pl.ds(pl.multiple_of(n * TILE, TILE), TILE)
            adj[at, cut_of(h)] = both(t_pair, at, c_pair.at[2 + h])

        for n in range(tiles - 1):
            add_partial(h, n)

    def finish(table, late, factor):
        h = pick(place, table)
        k = 2 * j + h
        late_got = lambda r: where(place, late, lambda: got(k, r)) if late else None

        @pl.loop(0, PIECES - 1)
        def _(r):
            late_got(r)
            at = pl.ds(pl.multiple_of(r * tall, tall), tall)
            grad[at, :] = factor * (grad[at, :] + product(k, at))
            adj[:, cut_of(h)] += lax.dot_general(
                t_own[at, :], c_all[k, at, :], (((0,), (0,)), ((), ())),
                preferred_element_type=jnp.float32,
            )

        late_got(PIECES - 1)
        p_copy(h, tiles - 1).wait_recv()

    def sent(send, bit):
        counts = [0] * 8
        for kind, *rest in PLAN:
            if kind == "hop":
                for i, entry in enumerate(rest[0]):
                    counts[i] += int(entry >= 0 and entry // bit % 2 == 1)
        rows = tall * half * 2 // (following * 4)
        for count in sorted(set(counts) - {0}):
            part = grad.at[pl.ds(0, count * rows)]
            places = tuple(i for i in range(8) if counts[i] == count)
            where(place, places, lambda: remote(part, part, send, send, partner).wait_send())

    def drain():
        block = c_all.at[pl.ds(0, 2)]

        def own_sent(send):
            remote(block, block, send, send, partner).wait_send()

        own_sent(own_send)
        pl.when(z == 1)(lambda: own_sent(own_extra.at[0]))
        pl.when(is_b)(lambda: own_sent(own_extra.at[1]))
        for r in range(AHEAD):
            pl.when(is_a & (z == 1))(lambda: own_ahead(0, r).wait_send())

        sent(down_send, 1)
        for i in range(4):
            pair_copy(i).wait_send()
        for h in range(2):
            v_across(h).wait_send()
            v_pair(h).wait_send()
        v_relay().wait_send()
        t_copy().wait_send()

    def begin_pairs():
        @pl.when(is_b)
        def _():
            for h, r in pairs:
                own_pair(h, r).start()

        t_copy().start()
        for h in range(2):
            v_pair(h).start()

    begun, ready, graded = False, False, False
    for kind, *rest in PLAN:
        if kind not in ("own", "v") and not begun:
            begun = True
            begin_pairs()
        if kind in ("part", "grad") and not ready:
            ready = True
            factor = jnp.max(discount_of(jnp.full((8, 128), section[0])))
            for copy in locals_:
                copy.wait()
            t_copy().wait_recv()
            for h in range(2):
                v_pair(h).wait_recv()
        if kind == "hop":
            hop(*rest)
        elif kind == "wait":
            bulk(*rest)
        elif kind == "own":
            own(*rest)
        elif kind == "v":
            where(place, rest[1], lambda: v_across(rest[0]).start())
        elif kind == "pair":
            where(place, rest[1], lambda: pair_copy(rest[0]).start())
        elif kind == "part":
            part(*rest)
        elif kind == "relay":
            for h in range(2):
                v_across(h).wait_recv()
            v_relay().start()
        elif kind == "v_q":
            where(place, rest[0], lambda: v_relay().wait_recv())
        elif kind == "grad":
            gradient(*rest, not graded)
            graded = True
        elif kind == "adj":
            adjoint(*rest, factor)
        elif kind == "pre":
            begin(*rest)
        else:
            drain()
            finish(*rest, factor)
            sent(up_send, 2)

    remote(p_out, p_out, p_send, p_send, partner).wait_send()


def stored(section, adj, grad, c_all, v_all, t_own, p_in, adj_out, grad_out, grad_last, adj_last, sems):
    m, s, u = (lax.axis_index(name) for name in ("markov", "storage", "sub"))
    place = 2 * (m + s * (3 - 2 * m)) + u + s * (1 - 2 * u)
    h = pick(place, PLAN[-1][1])
    k = 2 * (2 * s + u) + h
    states, half = c_all.shape[1:]
    kept = states - states // PIECES
    last = pl.ds(kept, states - kept)
    cut = pl.ds(pl.multiple_of(h * half, half), half)
    other = pl.ds(pl.multiple_of((1 - h) * half, half), half)
    copies = [
        pltpu.make_async_copy(grad.at[pl.ds(0, kept)], grad_out.at[pl.ds(0, kept)], sems.at[0]),
        pltpu.make_async_copy(adj.at[:, other], adj_out.at[:, other], sems.at[1]),
        pltpu.make_async_copy(grad_last, grad_out.at[last], sems.at[2]),
        pltpu.make_async_copy(adj_last, adj_out.at[:, cut], sems.at[3]),
    ]
    for copy in copies[:2]:
        copy.start()
    factor = jnp.max(discount_of(jnp.full((8, 128), section[0])))
    total = adj[:, cut] + lax.dot_general(
        t_own[last, :], c_all[k, last, :], (((0,), (0,)), ((), ())), preferred_element_type=jnp.float32
    )
    parts = decoded(p_in.at[h, p_in.shape[1] - 1])
    done = total.shape[0] - TILE
    adj_last[pl.ds(0, done), :] = factor * total[:done]
    tall = TILE // SHARE
    for i, part in enumerate(parts):
        top = done + i * tall
        adj_last[pl.ds(top, tall), :] = factor * (total[top : top + tall] + part)
    copies[3].start()
    grad_last[...] = factor * (
        grad[last, :]
        + lax.dot_general(
            c_all[k, last, :], v_all[k], (((1,), (1,)), ((), ())), preferred_element_type=jnp.float32
        )
    )
    copies[2].start()
    for copy in copies:
        copy.wait()


def exchanged(expected_cot, value_next, transition, section):
    states, cells = expected_cot.shape
    current, following = transition.shape
    dma = pltpu.SemaphoreType.DMA
    half = cells // 2
    tiles = following // TILE
    arrays = (expected_cot, value_next, transition)
    in_vmem = pl.BlockSpec(memory_space=pltpu.VMEM)
    in_hbm = pl.BlockSpec(memory_space=pltpu.HBM)
    in_smem = pl.BlockSpec(memory_space=pltpu.SMEM)
    outs = (
        jax.ShapeDtypeStruct((following, cells), jnp.float32),
        jax.ShapeDtypeStruct((current, following), jnp.float32),
    )
    held = (
        jax.ShapeDtypeStruct((8, states, half), jnp.bfloat16),
        jax.ShapeDtypeStruct((8, states, half), jnp.bfloat16),
        jax.ShapeDtypeStruct((current, following), jnp.bfloat16),
        jax.ShapeDtypeStruct((2, tiles, MESSAGE, half), jnp.int16),
    )
    sums = pl.pallas_call(
        kernel,
        out_shape=outs + held,
        in_specs=[in_smem] + [in_hbm] * 3,
        out_specs=(in_vmem,) * 6,
        scratch_shapes=[
            pltpu.VMEM((4, states, half), jnp.bfloat16),
            pltpu.VMEM((current, following), jnp.bfloat16),
            pltpu.VMEM((2, tiles, MESSAGE, half), jnp.int16),
            dma((8, PIECES)),
            dma,
            dma,
            dma,
            dma((3,)),
            dma((4,)),
            dma((4,)),
            dma((5,)),
            dma((5,)),
            dma((5,)),
            dma,
            dma((2, tiles)),
        ],
        compiler_params=pltpu.CompilerParams(
            collective_id=0, has_side_effects=True, vmem_limit_bytes=VMEM_BYTES
        ),
    )(section, *(pltpu.with_memory_space_constraint(x, pltpu.HBM) for x in arrays))
    return pl.pallas_call(
        stored,
        out_shape=outs,
        in_specs=[in_smem] + [in_vmem] * 6,
        out_specs=(in_hbm,) * 2,
        scratch_shapes=[
            pltpu.VMEM((states // PIECES, following), jnp.float32),
            pltpu.VMEM((following, half), jnp.float32),
            dma((4,)),
        ],
        compiler_params=pltpu.CompilerParams(vmem_limit_bytes=STORE_BYTES),
    )(section, *(pltpu.with_memory_space_constraint(x, pltpu.VMEM) for x in sums))


def solution(mesh):
    shape = mesh.shape
    paired = shape["storage"] == 2 and shape["sub"] == 2 and shape["markov"] == 4
    body = exchanged if paired else gathered
    return jax.shard_map(
        body,
        mesh=mesh,
        in_specs=(
            P(("groups", "markov"), ("storage", "sub")),
            P(("groups", "markov"), ("storage", "sub")),
            P(("groups", "storage", "sub"), "markov"),
            P("groups"),
        ),
        out_specs=(
            P(("groups", "markov"), ("storage", "sub")),
            P(("groups", "storage", "sub"), "markov"),
        ),
        check_vma=False,
    )
```
